256 devices in a mesh: trow: 32 (over z, x), tcol: 8 (over y, core).
Axes of the slice: x: 4, y: 4, z: 8, core: 2. Of those that a mesh axis runs over, the one named last changes fastest.
Arguments:
- query: bfloat16 [64, 512, 1152], P('trow', 'tcol'), may hold values from -64 to 64
- key: bfloat16 [64, 512, 1152], P('trow', 'tcol'), may hold values from -6 to 6
- value: bfloat16 [64, 512, 1152], P('trow', 'tcol'), may hold values from -6 to 6
- control: bfloat16 [64, 512, 1152], P('trow', 'tcol'), may hold values from -6 to 6
- kernel: float32 [3, 3, 1152], replicated, may hold values from -3 to 3
- grad_out: bfloat16 [64, 512, 1152], P('trow', 'tcol'), may hold values from -96 to 96
- detail_blocks: int32 [32, 8, 8], P('trow'), may hold values from -1 to 0, as said below
Outputs:
- grad_query: bfloat16 [64, 512, 1152], P('trow', 'tcol')
- grad_key: bfloat16 [64, 512, 1152], P('trow', 'tcol')
- grad_value: bfloat16 [64, 512, 1152], P('trow', 'tcol')
- grad_control: bfloat16 [64, 512, 1152], P('trow', 'tcol')
- grad_kernel: float32 [3, 3, 1152], replicated
The draws below stay inside these ranges and needn't reach their ends.
Inputs may be any that keep to these rules, and one draw needn't show every extreme that they name: `detail_blocks`: entry [i, j, p] is the key block of tile (i, p) that tile (i, j) also attends to, or -1 for none; entry [i, j, j] is -1; each tile names blocks of 1 to 7 other tiles, and in every tile row one tile names a block of each of the other 7 tiles.
All inputs are finite; a program needn't handle non-finite values.
Results may differ from the reference program's by a relative error of at most 0.0095.
Values may be sent and summed in bfloat16 or wider, within the bound.
A program may use at most 128 MiB of HBM per device.

```python
import jax
import jax.numpy as jnp
from jax import lax

HEADS = 16
HEAD_DIM = 72
D = 1152
TH = 2
TW = 64
BLOCK = 128
BLK_TILE = 1
TILE_ROWS = 32
TILE_COLS = 8
IMG_ROWS = 64
IMG_COLS = 512


def draw_key(key, part):
    shape = (IMG_ROWS, IMG_COLS, D)
    field = jnp.clip(jax.random.normal(jax.random.fold_in(key, 7), shape, jnp.float32), -6.0, 6.0)
    return field.astype(jnp.bfloat16)


def draw_query(key, part):
    shape = (IMG_ROWS, IMG_COLS, D)
    field = jnp.clip(jax.random.normal(jax.random.fold_in(key, 3), shape, jnp.float32), -6.0, 6.0)
    return field.astype(jnp.bfloat16)


def draw_detail_blocks(key, part):
    count_key = jax.random.fold_in(key, 31)
    full_key = jax.random.fold_in(key, 32)
    order_key = jax.random.fold_in(key, 33)
    block_key = jax.random.fold_in(key, 34)
    shape = (TILE_ROWS, TILE_COLS, TILE_COLS)
    counts = jnp.minimum(1 + jax.random.randint(count_key, (TILE_ROWS, TILE_COLS), 0, 4), TILE_COLS - 1)
    full_col = jax.random.randint(full_key, (TILE_ROWS,), 0, TILE_COLS)
    columns = jnp.arange(TILE_COLS, dtype=jnp.int32)
    counts = jnp.where(columns[None, :] == full_col[:, None], TILE_COLS - 1, counts)
    ranking = jax.random.randint(order_key, shape, 0, 1 << 20) * TILE_COLS + columns[None, None, :]
    itself = columns[:, None] == columns[None, :]
    ranking = jnp.where(itself[None, :, :], 1 << 30, ranking)
    places = jnp.argsort(jnp.argsort(ranking, axis=-1), axis=-1)
    picked = places < counts[:, :, None]
    blocks = jax.random.randint(block_key, shape, 0, BLK_TILE)
    return jnp.where(picked, blocks, -1).astype(jnp.int32)


def level_of(own_key, shape, cuts, low, largest):
    def one(axis_at, shards_of):
        steps = jax.random.uniform(jax.random.fold_in(jax.random.fold_in(own_key, 6), axis_at), (shards_of,), jnp.float32, low / len(cuts), largest / len(cuts))
        return jnp.repeat(jnp.exp(steps), shape[axis_at] // shards_of).reshape((-1,) + (1,) * (len(shape) - axis_at - 1))

    loudness = one(*cuts[0])
    for cut in cuts[1:]:
        loudness = loudness * one(*cut)
    return loudness


def centred(rng, dims, spread, bound, shards=(), held_as=jnp.bfloat16):
    level = level_of(rng, dims, shards, -0.22, 0.18) if shards else 1.0
    values = jax.random.normal(rng, dims, jnp.float32) * spread * level
    return jnp.minimum(jnp.maximum(values, -bound), bound).astype(held_as)


def setup_inputs(seed: int = 0) -> dict:
    seeds = jax.random.split(jax.random.key(seed), 8)
    return {
        "query": draw_query(jax.random.fold_in(seeds[7], 71), 0),
        "key": draw_key(jax.random.fold_in(seeds[7], 71), 0),
        "value": centred(seeds[2], (IMG_ROWS, IMG_COLS, D), 1.0, 6.0, ((0, 32), (1, 8))),
        "control": centred(seeds[3], (IMG_ROWS, IMG_COLS, D), 1.0, 6.0, ((0, 32), (1, 8))),
        "kernel": centred(seeds[4], (3, 3, D), 0.5, 3.0, (), jnp.float32),
        "grad_out": centred(seeds[5], (IMG_ROWS, IMG_COLS, D), 16.0, 96.0, ((0, 32), (1, 8))),
        "detail_blocks": draw_detail_blocks(jax.random.fold_in(seeds[7], 71), 0),
    }


NEG = -1e30


def rounded(values):
    narrow = values.astype(jnp.bfloat16)
    narrow = lax.optimization_barrier(narrow)
    return narrow.astype(jnp.float32)


def conv_taps(padded, kernel, rows, cols):
    total = jnp.zeros((rows, cols, padded.shape[2]), jnp.float32)
    for row_off in range(3):
        for col_off in range(3):
            total = total + kernel[row_off, col_off][None, None, :] * padded[row_off:row_off + rows, col_off:col_off + cols]
    return total


def conv_back(padded, kernel, rows, cols):
    total = jnp.zeros((rows, cols, padded.shape[2]), jnp.float32)
    for row_off in range(3):
        for col_off in range(3):
            total = total + kernel[row_off, col_off][None, None, :] * padded[2 - row_off:2 - row_off + rows, 2 - col_off:2 - col_off + cols]
    return total


def to_tiles(image, row_count, col_count):
    rows, cols, channels = image.shape
    tiled = image.reshape(row_count, rows // row_count, col_count, cols // col_count, channels)
    return tiled.transpose(0, 2, 1, 3, 4).reshape(row_count, col_count, (rows // row_count) * (cols // col_count), channels)


def from_tiles(tiles, tile_rows, tile_column_count):
    row_count, col_count, _, channels = tiles.shape
    image = tiles.reshape(row_count, col_count, tile_rows, tile_column_count, channels).transpose(0, 2, 1, 3, 4)
    return image.reshape(row_count * tile_rows, col_count * tile_column_count, channels)


def attend(queries, grads, keys, values, key_live):
    inv_root = HEAD_DIM ** -0.5
    q_three = queries.astype(jnp.float32).reshape(-1, HEADS, HEAD_DIM)
    g_three = grads.astype(jnp.float32).reshape(-1, HEADS, HEAD_DIM)
    k_three = keys.astype(jnp.float32).reshape(-1, HEADS, HEAD_DIM)
    value_three_axes = values.astype(jnp.float32).reshape(-1, HEADS, HEAD_DIM)
    scores = jnp.einsum("qhd,khd->hqk", q_three, k_three) * inv_root
    scores = jnp.where(key_live[None, None, :], scores, NEG)
    row_top = jnp.max(scores, axis=2, keepdims=True)
    raised = jnp.exp(scores - row_top)
    weights = raised / jnp.sum(raised, axis=2, keepdims=True)
    weights_bf = rounded(weights)
    attn_out = jnp.einsum("hqk,khd->qhd", weights_bf, value_three_axes)
    row_delta = jnp.sum(g_three * attn_out, axis=2)
    grad_weights = jnp.einsum("qhd,khd->hqk", g_three, value_three_axes)
    grad_scores = weights * (grad_weights - jnp.transpose(row_delta)[:, :, None])
    grad_scores_bf = rounded(grad_scores)
    grad_q = jnp.einsum("hqk,khd->qhd", grad_scores_bf, k_three) * inv_root
    grad_k = jnp.einsum("hqk,qhd->khd", grad_scores_bf, q_three) * inv_root
    grad_v = jnp.einsum("hqk,qhd->khd", weights_bf, g_three)
    channels = HEADS * HEAD_DIM
    return grad_q.reshape(-1, channels), grad_k.reshape(-1, channels), grad_v.reshape(-1, channels)


def add_tile(accum, piece, tile_row, tile_col, start):
    place = (jnp.asarray(tile_row, jnp.int32), jnp.asarray(tile_col, jnp.int32), jnp.asarray(start, jnp.int32), jnp.zeros((), jnp.int32))
    current = lax.dynamic_slice(accum, place, (1, 1, piece.shape[0], piece.shape[1]))
    return lax.dynamic_update_slice(accum, current + piece[None, None], place)


def reference(query, key, value, control, kernel, grad_out, detail_blocks):
    row_count = TILE_ROWS
    col_count = TILE_COLS
    tile_tokens = TH * TW
    channels = query.shape[2]
    control_pad = jnp.pad(control.astype(jnp.float32), ((1, 1), (1, 1), (0, 0)))
    control_conv = conv_taps(control_pad, kernel, IMG_ROWS, IMG_COLS)
    v_ctrl = (value.astype(jnp.float32) + control_conv).astype(jnp.bfloat16)
    q_tiles = to_tiles(query, row_count, col_count)
    key_tile_stack = to_tiles(key, row_count, col_count)
    v_tiles = to_tiles(v_ctrl, row_count, col_count)
    g_tiles = to_tiles(grad_out, row_count, col_count)
    k_pad = jnp.pad(key_tile_stack, ((1, 1), (0, 0), (0, 0), (0, 0)))
    v_pad = jnp.pad(v_tiles, ((1, 1), (0, 0), (0, 0), (0, 0)))
    zero_acc = jnp.zeros((row_count + 2, col_count, tile_tokens, channels), jnp.float32)

    def visit(carry, index):
        key_acc, value_running_sum = carry
        my_row = index // col_count
        my_col = index % col_count
        key_parts = [k_pad[my_row + 1, my_col], k_pad[my_row, my_col], k_pad[my_row + 2, my_col]]
        value_parts = [v_pad[my_row + 1, my_col], v_pad[my_row, my_col], v_pad[my_row + 2, my_col]]
        live_parts = [jnp.ones((tile_tokens,), bool), jnp.full((tile_tokens,), my_row >= 1), jnp.full((tile_tokens,), my_row + 1 < row_count)]
        starts = []
        peers = []
        for slot in range(col_count - 1):
            peer = (slot + (slot >= my_col)).astype(jnp.int32)
            chosen = detail_blocks[my_row, my_col, peer]
            start = (jnp.maximum(chosen, 0) * BLOCK).astype(jnp.int32)
            key_parts.append(lax.dynamic_slice_in_dim(key_tile_stack[my_row, peer], start, BLOCK, 0))
            value_parts.append(lax.dynamic_slice_in_dim(v_tiles[my_row, peer], start, BLOCK, 0))
            live_parts.append(jnp.full((BLOCK,), chosen >= 0))
            starts.append(start)
            peers.append(peer)
        keys = jnp.concatenate(key_parts, axis=0)
        values = jnp.concatenate(value_parts, axis=0)
        key_live = jnp.concatenate(live_parts, axis=0)
        grad_q, grad_k, grad_v = attend(q_tiles[my_row, my_col], g_tiles[my_row, my_col], keys, values, key_live)
        zero_start = jnp.zeros((), jnp.int32)
        offsets = [(my_row + 1, 0), (my_row, tile_tokens), (my_row + 2, 2 * tile_tokens)]
        for tile_row, first in offsets:
            key_acc = add_tile(key_acc, grad_k[first:first + tile_tokens], tile_row, my_col, zero_start)
            value_running_sum = add_tile(value_running_sum, grad_v[first:first + tile_tokens], tile_row, my_col, zero_start)
        for slot in range(col_count - 1):
            first = 3 * tile_tokens + slot * BLOCK
            key_acc = add_tile(key_acc, rounded(grad_k[first:first + BLOCK]), my_row + 1, peers[slot], starts[slot])
            value_running_sum = add_tile(value_running_sum, rounded(grad_v[first:first + BLOCK]), my_row + 1, peers[slot], starts[slot])
        return (key_acc, value_running_sum), grad_q

    (key_acc, value_running_sum), q_grads = lax.scan(visit, (zero_acc, zero_acc), jnp.arange(row_count * col_count, dtype=jnp.int32))
    grad_query = from_tiles(q_grads.reshape(row_count, col_count, tile_tokens, channels), TH, TW).astype(jnp.bfloat16)
    grad_key = from_tiles(key_acc[1:row_count + 1], TH, TW).astype(jnp.bfloat16)
    grad_value = from_tiles(value_running_sum[1:row_count + 1], TH, TW).astype(jnp.bfloat16)
    grad_value_f = grad_value.astype(jnp.float32)
    value_pad = jnp.pad(grad_value_f, ((1, 1), (1, 1), (0, 0)))
    grad_control = conv_back(value_pad, kernel, IMG_ROWS, IMG_COLS).astype(jnp.bfloat16)
    kernel_rows = []
    for row_off in range(3):
        kernel_cols = []
        for col_off in range(3):
            kernel_cols.append(jnp.sum(control_pad[row_off:row_off + IMG_ROWS, col_off:col_off + IMG_COLS] * grad_value_f, axis=(0, 1)))
        kernel_rows.append(jnp.stack(kernel_cols, axis=0))
    grad_kernel = jnp.stack(kernel_rows, axis=0)
    return grad_query, grad_key, grad_value, grad_control, grad_kernel
```

```python
import functools
import math

import jax
import jax.numpy as jnp
from jax import lax
from jax.experimental import pallas as pl
from jax.experimental.pallas import tpu as pltpu
from jax.sharding import PartitionSpec as P

HEADS = 16
HEAD_DIM = 72
PAD_DIM = 80
D = 1152
TOK = 128
NX = 4
NY = 4
TR = 32
TC = 8
NZ = TR // NX
LANES = D // 128
ROOT = HEAD_DIM ** (-0.5)
EXP_SCALE = ROOT * math.log2(math.e)
BIG = 1e30
MESH = pl.DeviceIdType.MESH
F32 = jnp.float32
BF16 = jnp.bfloat16
DIRS = ((-1, -1), (-1, 0), (-1, 1), (0, -1), (0, 1), (1, -1), (1, 0), (1, 1))


class Place:
    def __init__(self):
        self.tr = lax.axis_index("trow")
        self.tc = lax.axis_index("tcol")
        self.z = self.tr // NX
        self.x = self.tr % NX
        self.y = self.tc // 2
        self.c = self.tc % 2
        self.u = 2 * self.z + self.c

    def chain(self, step):
        u = self.u + step
        return (NX * (u // 2) + self.x, 2 * self.y + u % 2)

    def has_chain(self, step):
        u = self.u + step
        return (u >= 0) & (u < 2 * NZ)

    def has_dir(self, dr, dc):
        r = self.tr + dr
        c = self.tc + dc
        return (r >= 0) & (r < TR) & (c >= 0) & (c < TC)


def signal(sem, dev):
    pl.semaphore_signal(sem, inc=1, device_id=dev, device_id_type=MESH)


def entry_barrier(me, with_z):
    bar = pltpu.get_barrier_semaphore()
    total = jnp.int32(NX * TC - 1)
    for step in range(1, NX * TC):
        rank = (me.x * TC + me.tc + step) % (NX * TC)
        signal(bar, (NX * me.z + rank // TC, rank % TC))
    for step in (-1, 1):
        ok = me.has_chain(step)
        total = total + ok.astype(jnp.int32)

        @pl.when(ok)
        def _():
            signal(bar, me.chain(step))

    for dr, dc in DIRS:
        ok = me.has_dir(dr, dc)
        total = total + ok.astype(jnp.int32)

        @pl.when(ok)
        def _():
            signal(bar, (me.tr + dr, me.tc + dc))

    if with_z:
        for step in range(1, NZ):
            zz = (me.z + step) % NZ
            signal(bar, (NX * zz + me.x, me.tc))
        total = total + (NZ - 1)
    pl.semaphore_wait(bar, total)


def remote(src, dst, ssem, rsem, dev):
    return pltpu.make_async_remote_copy(
        src_ref=src, dst_ref=dst, send_sem=ssem, recv_sem=rsem, device_id=dev, device_id_type=MESH
    )


def start_or_local(is_self, src, dst, ssem, rsem, dev):
    @pl.when(is_self)
    def _():
        pltpu.make_async_copy(src, dst, rsem).start()

    @pl.when(jnp.logical_not(is_self))
    def _():
        remote(src, dst, ssem, rsem, dev).start()


def wait_sent(is_self, src, dst, ssem, rsem, dev):
    @pl.when(jnp.logical_not(is_self))
    def _():
        remote(src, dst, ssem, rsem, dev).wait_send()


def wait_bytes(ref, sem):
    pltpu.make_async_copy(ref, ref, sem).wait()


def halo_views(img, rows, cols, diag, dr, dc):
    row = 0 if dr < 0 else 1
    col = 0 if dc < 0 else 48
    if dc == 0:
        return img.at[row], rows.at[1 if dr < 0 else 0]
    if dr == 0:
        return img.at[:, pl.ds(col, 16), :], cols.at[1 if dc < 0 else 0]
    slot = (2 if dr < 0 else 0) + (1 if dc < 0 else 0)
    return img.at[row, pl.ds(col, 16), :], diag.at[slot]


def halo_start(me, img, rows, cols, diag, ssem, rsem):
    for at, (dr, dc) in enumerate(DIRS):
        src, dst = halo_views(img, rows, cols, diag, dr, dc)

        @pl.when(me.has_dir(dr, dc))
        def _():
            remote(src, dst, ssem.at[at], rsem.at[at], (me.tr + dr, me.tc + dc)).start()


def halo_wait(me, img, rows, cols, diag, ssem, rsem):
    for at, (dr, dc) in enumerate(DIRS):
        src, dst = halo_views(img, rows, cols, diag, dr, dc)

        @pl.when(me.has_dir(dr, dc))
        def _():
            remote(src, dst, ssem.at[at], rsem.at[at], (me.tr + dr, me.tc + dc)).wait_send()

        @pl.when(me.has_dir(-dr, -dc))
        def _():
            remote(src, dst, ssem.at[at], rsem.at[at], (me.tr - dr, me.tc - dc)).wait_recv()


def fill_ext(me, ext, img, rows, cols, diag):
    ext[1:3, 8:72, :] = img[...].astype(F32)
    up = me.has_dir(-1, 0)
    down = me.has_dir(1, 0)
    left = me.has_dir(0, -1)
    right = me.has_dir(0, 1)

    def put(ok, place, value):
        ext[place] = jnp.where(ok, value.astype(F32), 0.0)

    put(up, (0, slice(8, 72)), rows[0])
    put(down, (3, slice(8, 72)), rows[1])
    for r in range(2):
        put(left, (1 + r, slice(0, 8)), cols[0, r].astype(F32)[8:16])
        put(right, (1 + r, slice(72, 80)), cols[1, r].astype(F32)[0:8])
    put(up & left, (0, slice(0, 8)), diag[0].astype(F32)[8:16])
    put(up & right, (0, slice(72, 80)), diag[1].astype(F32)[0:8])
    put(down & left, (3, slice(0, 8)), diag[2].astype(F32)[8:16])
    put(down & right, (3, slice(72, 80)), diag[3].astype(F32)[0:8])


def to_heads(x, flip, out):
    for b in range(LANES):
        flip[pl.ds(b * 128, 128), :] = x(b).T
    zero = jnp.zeros((PAD_DIM - HEAD_DIM, TOK), F32)
    for h in range(HEADS):
        out[h] = jnp.concatenate([flip[pl.ds(h * HEAD_DIM, HEAD_DIM), :], zero], axis=0).astype(BF16)


def scatter_kernel(
    q, k, v, g, c, w, db,
    oq, og, ok, ov, om, oext,
    sq, sg, sk, sv, sm, flip, hrow, hcol, hdiag,
    asend, arecv, msend, mrecv, bsend, brecv, hsend, hrecv,
):
    me = Place()
    for p in range(TC):
        live = (db[0, me.tc, p] >= 0) | (me.tc == p)
        sm[pl.ds(p, 1), :] = jnp.full((1, TOK), jnp.where(live, 0.0, BIG), F32)
    entry_barrier(me, False)
    halo_start(me, c, hrow, hcol, hdiag, hsend, hrecv)
    r = me.x % 2

    def dest(h):
        dev = (NX * me.z + h // NY, 2 * (h % NY) + me.x // 2)
        return dev, (dev[0] == me.tr) & (dev[1] == me.tc)

    def head_copies(act, n, src, dst):
        for h in range(HEADS):
            dev, is_self = dest(h)
            act(is_self, src.at[h], dst.at[r, me.tc], asend.at[n, h], arecv.at[n, r], dev)

    def mask_copies(act):
        for h in range(HEADS):
            dev, is_self = dest(h)
            act(is_self, sm, om.at[r, me.tc], msend.at[h], mrecv, dev)

    own_k = ok.at[pl.ds(1, 2)]
    own_v = ov.at[pl.ds(1, 2)]
    to_heads(lambda b: k[:, :, b * 128 : b * 128 + 128].reshape(TOK, 128).astype(F32), flip, sk)
    head_copies(start_or_local, 0, sk, own_k)
    mask_copies(start_or_local)
    to_heads(lambda b: q[:, :, b * 128 : b * 128 + 128].reshape(TOK, 128).astype(F32), flip, sq)
    head_copies(start_or_local, 1, sq, oq)
    halo_wait(me, c, hrow, hcol, hdiag, hsend, hrecv)
    fill_ext(me, oext, c, hrow, hcol, hdiag)

    def v_block(b):
        lanes = slice(b * 128, b * 128 + 128)
        total = v[:, :, lanes].astype(F32)
        for a in range(3):
            for s in range(3):
                total = total + w[a, s, lanes][None, None, :] * oext[a : a + 2, 7 + s : 71 + s, lanes]
        return total.astype(BF16).astype(F32).reshape(TOK, 128)

    to_heads(v_block, flip, sv)
    head_copies(start_or_local, 2, sv, own_v)
    to_heads(lambda b: g[:, :, b * 128 : b * 128 + 128].reshape(TOK, 128).astype(F32), flip, sg)
    head_copies(start_or_local, 3, sg, og)

    def chain_copy(at, arr, buf, step):
        src, dst = (buf.at[1], buf.at[3]) if step < 0 else (buf.at[2], buf.at[0])
        return remote(src, dst, bsend.at[arr, at], brecv.at[arr, at], me.chain(step))

    for n, arr, buf in ((0, 0, ok), (2, 1, ov)):
        for at, step in enumerate((-1, 1)):
            wait_bytes(buf.at[1 + at], arecv.at[n, at])

            @pl.when(me.has_chain(step))
            def _():
                chain_copy(at, arr, buf, step).start()

        @pl.when(jnp.logical_not(me.has_chain(-1)))
        def _():
            buf[0] = jnp.zeros(buf.shape[1:], BF16)

        @pl.when(jnp.logical_not(me.has_chain(1)))
        def _():
            buf[3] = jnp.zeros(buf.shape[1:], BF16)

    for n, buf in ((1, oq), (3, og)):
        for at in range(2):
            wait_bytes(buf.at[at], arecv.at[n, at])
    wait_bytes(om, mrecv)
    for n, src, dst in ((0, sk, own_k), (1, sq, oq), (2, sv, own_v), (3, sg, og)):
        head_copies(wait_sent, n, src, dst)
    mask_copies(wait_sent)
    for arr, buf in ((0, ok), (1, ov)):
        for at, step in enumerate((-1, 1)):

            @pl.when(me.has_chain(step))
            def _():
                chain_copy(at, arr, buf, step).wait_send()

            @pl.when(me.has_chain(-step))
            def _():
                chain_copy(at, arr, buf, step).wait_recv()


def dot(a, b, ca, cb):
    return lax.dot_general(a, b, (((ca,), (cb,)), ((), ())), preferred_element_type=F32)


def attend_kernel(q, g, k, v, m, odq, odk, odv, kt, vt, s_buf, t_buf):
    me = Place()
    odk[...] = jnp.zeros(odk.shape, F32)
    odv[...] = jnp.zeros(odv.shape, F32)

    def flip_one(i, _):
        a = i // TC
        j = i % TC
        kt[a, j] = k[a, j].astype(F32).T.astype(BF16)
        vt[a, j] = v[a, j].astype(F32).T.astype(BF16)
        return 0

    lax.fori_loop(0, 4 * TC, flip_one, 0)

    def visit(i, _):
        r = i // (TC // 2)
        j = 2 * (i % (TC // 2))
        qs = [q[r, j], q[r, j + 1]]
        gs = [g[r, j], g[r, j + 1]]
        q2 = jnp.concatenate(qs, axis=1)
        g2 = jnp.concatenate(gs, axis=1)
        bias = []
        for p in range(TC):
            bias.append(jnp.concatenate([m[r, j, pl.ds(p, 1), :], m[r, j + 1, pl.ds(p, 1), :]], axis=1))
        above_dead = (me.u == 0) & (r == 0)
        below_dead = (me.u == 2 * NZ - 1) & (r == 1)
        for dead in (above_dead, below_dead):
            bias.append(jnp.full((1, 2 * TOK), jnp.where(dead, BIG, 0.0), F32))
        top = jnp.full((8, 2 * TOK), -3.0e38, F32)
        for p in range(TC + 2):
            if p < TC:
                s = dot(kt[1 + r, p], q2, 1, 0)
            else:
                a = r + 2 * (p - TC)
                s = jnp.concatenate([dot(kt[a, j + t], qs[t], 1, 0) for t in range(2)], axis=1)
            s_buf[p] = s
            top = jnp.maximum(top, jnp.max(s.reshape(TOK // 8, 8, 2 * TOK), axis=0) - bias[p])
        top = jnp.max(top, axis=0, keepdims=True) * EXP_SCALE
        total = jnp.zeros((8, 2 * TOK), F32)
        delta = jnp.zeros((8, 2 * TOK), F32)
        for p in range(TC + 2):
            e = jnp.exp2(s_buf[p] * EXP_SCALE - (top + bias[p]))
            if p < TC:
                gw = dot(vt[1 + r, p], g2, 1, 0)
            else:
                a = r + 2 * (p - TC)
                gw = jnp.concatenate([dot(vt[a, j + t], gs[t], 1, 0) for t in range(2)], axis=1)
            te = e * gw
            s_buf[p] = e
            t_buf[p] = te
            total = total + jnp.sum(e.reshape(TOK // 8, 8, 2 * TOK), axis=0)
            delta = delta + jnp.sum(te.reshape(TOK // 8, 8, 2 * TOK), axis=0)
        inv = 1.0 / jnp.sum(total, axis=0, keepdims=True)
        delta = jnp.sum(delta, axis=0, keepdims=True) * inv
        qn = (q2.astype(F32) * (inv * ROOT)).astype(BF16)
        gn = (g2.astype(F32) * inv).astype(BF16)
        dq = jnp.zeros((PAD_DIM, 2 * TOK), F32)
        for p in range(TC + 2):
            e = s_buf[p]
            ds = (t_buf[p] - e * delta).astype(BF16)
            eb = e.astype(BF16)
            if p < TC:
                dq = dq + dot(k[1 + r, p], ds, 1, 0)
                odk[1 + r, p] += dot(qn, ds, 1, 1)
                odv[1 + r, p] += dot(gn, eb, 1, 1)
            else:
                a = r + 2 * (p - TC)
                parts = []
                for t in range(2):
                    half = slice(t * TOK, (t + 1) * TOK)
                    parts.append(dot(k[a, j + t], ds[:, half], 1, 0))
                    odk[a, j + t] += dot(qn[:, half], ds[:, half], 1, 1)
                    odv[a, j + t] += dot(gn[:, half], eb[:, half], 1, 1)
                dq = dq + jnp.concatenate(parts, axis=1)
        dq = (dq * (inv * ROOT)).astype(BF16)
        odq[r, j] = dq[:, :TOK]
        odq[r, j + 1] = dq[:, TOK:]
        return 0

    lax.fori_loop(0, TC, visit, 0)


def from_heads(land, flip, put):
    for h in range(HEADS):
        flip[pl.ds(h * HEAD_DIM, HEAD_DIM), :] = land[h].astype(F32)[:HEAD_DIM]
    for b in range(LANES):
        put(b, flip[pl.ds(b * 128, 128), :].T)


def gather_kernel(
    dq, dk, dv, cext, w,
    oq, ok, ov, oc, ow,
    edge, elan, sk, sv, lq, lk, lv, flip, ext, hrow, hcol, hdiag,
    pieces, red1, red2, red3, red4, part2, part3, part4,
    csend, crecv, asend, arecv, hsend, hrecv, psend, precv,
):
    me = Place()
    for arr, src in ((0, dk), (1, dv)):
        edge[arr, 0] = src[0].astype(BF16)
        edge[arr, 1] = src[3].astype(BF16)
    entry_barrier(me, True)

    def chain_copy(arr, at, step):
        return remote(edge.at[arr, at], elan.at[arr, 1 - at], csend.at[arr, at], crecv.at[arr, at], me.chain(step))

    order = (1, 0)
    for arr in order:
        for at, step in enumerate((-1, 1)):

            @pl.when(me.has_chain(step))
            def _():
                chain_copy(arr, at, step).start()

    head = me.x * NY + me.y

    def tile_copies(act, n, src, dst):
        for r in range(2):
            for j in range(TC):
                dev = (NX * me.z + 2 * me.c + r, j)
                is_self = (dev[0] == me.tr) & (me.tc == j)
                act(is_self, src.at[r, j], dst.at[head], asend.at[n, r * TC + j], arecv.at[n], dev)

    tile_copies(start_or_local, 0, dq, lq)
    for arr, n, acc, out, land in ((1, 2, dv, sv, lv), (0, 1, dk, sk, lk)):
        for at, step in enumerate((-1, 1)):
            @pl.when(me.has_chain(-step))
            def _():
                chain_copy(arr, at, step).wait_recv()

            row = 1 - at
            ok_here = me.has_chain(-step)
            extra = jnp.where(ok_here, elan[arr, row].astype(F32), 0.0)
            out[row] = (acc[1 + row] + extra).astype(BF16)
        tile_copies(start_or_local, n, out, land)

    def out_block(out):
        def put(b, x):
            out[:, :, b * 128 : b * 128 + 128] = x.reshape(2, 64, 128).astype(BF16)

        return put

    wait_bytes(lq, arecv.at[0])
    from_heads(lq, flip, out_block(oq))
    wait_bytes(lv, arecv.at[2])
    from_heads(lv, flip, out_block(ov))
    halo_start(me, ov, hrow, hcol, hdiag, hsend, hrecv)
    for b in range(LANES):
        lanes = slice(b * 128, b * 128 + 128)
        gv = ov[:, :, lanes].astype(F32)
        for a in range(3):
            for s in range(3):
                prod = gv * cext[a : a + 2, 7 + s : 71 + s, lanes]
                t = (a * 3 + s) * LANES + b
                pieces[t // 11, pl.ds(t % 11, 1), :] = jnp.sum(prod.reshape(TOK, 128), axis=0, keepdims=True)

    def exchange(stage, count, mine, src, land, dev):
        def run(act):
            for other in range(count):
                view = src.at[other] if stage == 0 else src
                act(mine == other, view, land.at[mine], psend.at[stage, other], precv.at[stage], dev(other))

        run(start_or_local)
        return run

    runs = []
    runs.append(exchange(0, TC, me.tc, pieces, red1, lambda o: (me.tr, o)))
    wait_bytes(lk, arecv.at[1])
    from_heads(lk, flip, out_block(ok))
    wait_bytes(red1, precv.at[0])
    part2[...] = jnp.sum(red1[...], axis=0)
    runs.append(exchange(1, NX, me.x, part2, red2, lambda o: (NX * me.z + o, me.tc)))
    halo_wait(me, ov, hrow, hcol, hdiag, hsend, hrecv)
    fill_ext(me, ext, ov, hrow, hcol, hdiag)
    wait_bytes(red2, precv.at[1])
    part3[...] = jnp.sum(red2[...], axis=0)
    runs.append(exchange(2, NZ, me.z, part3, red3, lambda o: (NX * o + me.x, me.tc)))
    for b in range(LANES):
        lanes = slice(b * 128, b * 128 + 128)
        total = jnp.zeros((2, 64, 128), F32)
        for a in range(3):
            for s in range(3):
                total = total + w[a, s, lanes][None, None, :] * ext[2 - a : 4 - a, 9 - s : 73 - s, lanes]
        oc[:, :, lanes] = total.astype(BF16)
    wait_bytes(red3, precv.at[2])
    part4[...] = jnp.sum(red3[...], axis=0)
    runs.append(exchange(3, TC, me.tc, part4, red4, lambda o: (me.tr, o)))
    tile_copies(wait_sent, 0, dq, lq)
    tile_copies(wait_sent, 1, sk, lk)
    tile_copies(wait_sent, 2, sv, lv)
    for arr in order:
        for at, step in enumerate((-1, 1)):

            @pl.when(me.has_chain(step))
            def _():
                chain_copy(arr, at, step).wait_send()

    wait_bytes(red4, precv.at[3])
    for t in range(9 * LANES):
        tap, b = t // LANES, t % LANES
        ow[tap // 3, pl.ds(tap % 3, 1), b * 128 : b * 128 + 128] = red4[t // 11, pl.ds(t % 11, 1), :]
    for run in runs:
        run(wait_sent)


def vmem_specs(n):
    return [pl.BlockSpec(memory_space=pltpu.VMEM)] * n


def per_device(query, key, value, control, kernel, grad_out, detail_blocks):
    sds = jax.ShapeDtypeStruct
    heads = lambda n: sds((n, TC, PAD_DIM, TOK), BF16)
    sem = pltpu.SemaphoreType.DMA
    vm = pltpu.VMEM
    qh, gh, kh, vh, mask, cext = pl.pallas_call(
        scatter_kernel,
        out_shape=(heads(2), heads(2), heads(4), heads(4), sds((2, TC, 8, TOK), F32), sds((4, 80, D), F32)),
        in_specs=vmem_specs(6) + [pl.BlockSpec(memory_space=pltpu.SMEM)],
        out_specs=tuple(vmem_specs(6)),
        scratch_shapes=[vm((HEADS, PAD_DIM, TOK), BF16)] * 4
        + [vm((8, TOK), F32), vm((D, TOK), F32)]
        + [vm((2, 64, D), BF16), vm((2, 2, 16, D), BF16), vm((4, 16, D), BF16)]
        + [sem((4, HEADS)), sem((4, 2)), sem((HEADS,)), sem, sem((2, 2)), sem((2, 2)), sem((8,)), sem((8,))],
        compiler_params=pltpu.CompilerParams(collective_id=0, has_side_effects=True),
        name="scatter",
    )(query, key, value, grad_out, control, kernel, detail_blocks)
    acc = sds((4, TC, PAD_DIM, TOK), F32)
    dq, dk, dv = pl.pallas_call(
        attend_kernel,
        out_shape=(heads(2), acc, acc),
        in_specs=vmem_specs(5),
        out_specs=tuple(vmem_specs(3)),
        scratch_shapes=[vm((4, TC, TOK, PAD_DIM), BF16)] * 2 + [vm((TC + 2, TOK, 2 * TOK), F32)] * 2,
        name="attend",
    )(qh, gh, kh, vh, mask)
    img = sds((2, 64, D), BF16)
    piece = vm((16, TOK), F32)
    gq, gk, gv, gc, gw = pl.pallas_call(
        gather_kernel,
        out_shape=(img, img, img, img, sds((3, 3, D), F32)),
        in_specs=vmem_specs(5),
        out_specs=tuple(vmem_specs(5)),
        scratch_shapes=[vm((2, 2, TC, PAD_DIM, TOK), BF16)] * 2
        + [vm((2, TC, PAD_DIM, TOK), BF16)] * 2
        + [vm((HEADS, PAD_DIM, TOK), BF16)] * 3
        + [vm((D, TOK), F32), vm((4, 80, D), F32)]
        + [vm((2, 64, D), BF16), vm((2, 2, 16, D), BF16), vm((4, 16, D), BF16)]
        + [vm((TC, 16, TOK), F32), vm((TC, 16, TOK), F32), vm((NX, 16, TOK), F32), vm((NZ, 16, TOK), F32), vm((TC, 16, TOK), F32)]
        + [piece] * 3
        + [sem((2, 2)), sem((2, 2)), sem((3, HEADS)), sem((3,)), sem((8,)), sem((8,)), sem((4, 8)), sem((4,))],
        compiler_params=pltpu.CompilerParams(collective_id=1, has_side_effects=True),
        name="gather",
    )(dq, dk, dv, cext, kernel)
    return gq, gk, gv, gc, gw


def solution(mesh):
    tile = P("trow", "tcol", None)
    return jax.shard_map(
        per_device,
        mesh=mesh,
        in_specs=(tile, tile, tile, tile, P(), tile, P("trow", None, None)),
        out_specs=(tile, tile, tile, tile, P()),
        check_vma=False,
    )
```

```python
import functools
import math

import jax
import jax.numpy as jnp
from jax import lax
from jax.experimental import pallas as pl
from jax.experimental.pallas import tpu as pltpu
from jax.sharding import PartitionSpec as P

HEADS = 16
HEAD_DIM = 72
PAD_DIM = 80
D = 1152
TOK = 128
NX = 4
NY = 4
TR = 32
TC = 8
NZ = TR // NX
LANES = D // 128
ROOT = HEAD_DIM ** (-0.5)
EXP_SCALE = ROOT * math.log2(math.e)
BIG = 1e30
MESH = pl.DeviceIdType.MESH
F32 = jnp.float32
BF16 = jnp.bfloat16
DIRS = ((-1, -1), (-1, 0), (-1, 1), (0, -1), (0, 1), (1, -1), (1, 0), (1, 1))


class Place:
    def __init__(self):
        self.tr = lax.axis_index("trow")
        self.tc = lax.axis_index("tcol")
        self.z = self.tr // NX
        self.x = self.tr % NX
        self.y = self.tc // 2
        self.c = self.tc % 2
        self.u = 2 * self.z + self.c

    def chain(self, step):
        u = self.u + step
        return (NX * (u // 2) + self.x, 2 * self.y + u % 2)

    def has_chain(self, step):
        u = self.u + step
        return (u >= 0) & (u < 2 * NZ)

    def has_dir(self, dr, dc):
        r = self.tr + dr
        c = self.tc + dc
        return (r >= 0) & (r < TR) & (c >= 0) & (c < TC)


def signal(sem, dev):
    pl.semaphore_signal(sem, inc=1, device_id=dev, device_id_type=MESH)


def greet(me):
    bar = pltpu.get_barrier_semaphore()
    total = jnp.int32(NX * TC - 1)
    for step in range(1, NX * TC):
        rank = (me.x * TC + me.tc + step) % (NX * TC)
        signal(bar, (NX * me.z + rank // TC, rank % TC))
    for step in (-1, 1):
        ok = me.has_chain(step)
        total = total + ok.astype(jnp.int32)

        @pl.when(ok)
        def _():
            signal(bar, me.chain(step))

    for dr, dc in DIRS:
        ok = me.has_dir(dr, dc)
        total = total + ok.astype(jnp.int32)

        @pl.when(ok)
        def _():
            signal(bar, (me.tr + dr, me.tc + dc))

    for step in range(1, NZ):
        signal(bar, (NX * ((me.z + step) % NZ) + me.x, me.tc))
    return bar, total + (NZ - 1)


def remote(src, dst, ssem, rsem, dev):
    return pltpu.make_async_remote_copy(
        src_ref=src, dst_ref=dst, send_sem=ssem, recv_sem=rsem, device_id=dev, device_id_type=MESH
    )


def start_or_local(is_self, src, dst, ssem, rsem, dev):
    @pl.when(is_self)
    def _():
        pltpu.make_async_copy(src, dst, rsem).start()

    @pl.when(jnp.logical_not(is_self))
    def _():
        remote(src, dst, ssem, rsem, dev).start()


def wait_sent(is_self, src, dst, ssem, rsem, dev):
    @pl.when(jnp.logical_not(is_self))
    def _():
        remote(src, dst, ssem, rsem, dev).wait_send()


def wait_bytes(ref, sem):
    pltpu.make_async_copy(ref, ref, sem).wait()


def halo_views(img, rows, cols, diag, dr, dc):
    row = 0 if dr < 0 else 1
    col = 0 if dc < 0 else 48
    if dc == 0:
        return img.at[row], rows.at[1 if dr < 0 else 0]
    if dr == 0:
        return img.at[:, pl.ds(col, 16), :], cols.at[1 if dc < 0 else 0]
    slot = (2 if dr < 0 else 0) + (1 if dc < 0 else 0)
    return img.at[row, pl.ds(col, 16), :], diag.at[slot]


def halo_start(me, img, rows, cols, diag, ssem, rsem):
    for at, (dr, dc) in enumerate(DIRS):
        src, dst = halo_views(img, rows, cols, diag, dr, dc)

        @pl.when(me.has_dir(dr, dc))
        def _():
            remote(src, dst, ssem.at[at], rsem.at[at], (me.tr + dr, me.tc + dc)).start()


def halo_wait(me, img, rows, cols, diag, ssem, rsem):
    for at, (dr, dc) in enumerate(DIRS):
        src, dst = halo_views(img, rows, cols, diag, dr, dc)

        @pl.when(me.has_dir(dr, dc))
        def _():
            remote(src, dst, ssem.at[at], rsem.at[at], (me.tr + dr, me.tc + dc)).wait_send()

        @pl.when(me.has_dir(-dr, -dc))
        def _():
            remote(src, dst, ssem.at[at], rsem.at[at], (me.tr - dr, me.tc - dc)).wait_recv()


def fill_ext(me, ext, img, rows, cols, diag):
    ext[1:3, 8:72, :] = img[...].astype(F32)
    up = me.has_dir(-1, 0)
    down = me.has_dir(1, 0)
    left = me.has_dir(0, -1)
    right = me.has_dir(0, 1)

    def put(ok, place, value):
        ext[place] = jnp.where(ok, value.astype(F32), 0.0)

    put(up, (0, slice(8, 72)), rows[0])
    put(down, (3, slice(8, 72)), rows[1])
    for r in range(2):
        put(left, (1 + r, slice(0, 8)), cols[0, r].astype(F32)[8:16])
        put(right, (1 + r, slice(72, 80)), cols[1, r].astype(F32)[0:8])
    put(up & left, (0, slice(0, 8)), diag[0].astype(F32)[8:16])
    put(up & right, (0, slice(72, 80)), diag[1].astype(F32)[0:8])
    put(down & left, (3, slice(0, 8)), diag[2].astype(F32)[8:16])
    put(down & right, (3, slice(72, 80)), diag[3].astype(F32)[0:8])


def to_heads(x, flip, out):
    for b in range(LANES):
        flip[pl.ds(b * 128, 128), :] = x(b).T
    zero = jnp.zeros((PAD_DIM - HEAD_DIM, TOK), F32)
    for h in range(HEADS):
        out[h] = jnp.concatenate([flip[pl.ds(h * HEAD_DIM, HEAD_DIM), :], zero], axis=0).astype(BF16)


def dot(a, b, ca, cb):
    return lax.dot_general(a, b, (((ca,), (cb,)), ((), ())), preferred_element_type=F32)


def from_heads(land, flip, put):
    for h in range(HEADS):
        flip[pl.ds(h * HEAD_DIM, HEAD_DIM), :] = land[h].astype(F32)[:HEAD_DIM]
    for b in range(LANES):
        put(b, flip[pl.ds(b * 128, 128), :].T)


def whole_kernel(
    q, k, v, g, c, w, db,
    oq, ok, ov, oc, ow,
    hq, hg, hk, hv, hm,
    sq, sg, sk, sv, sm, flip, ext, cext, hrow, hcol, hdiag, grow, gcol, gdiag,
    kt, vt, s_buf, t_buf, acc_k, acc_v, tq, tk, tv, edge, elan, lq, lk, lv,
    pieces, red1, red2, red3, red4, part2, part3, part4,
    asend, arecv, msend, mrecv, bsend, brecv, hsend, hrecv, gsend, grecv,
    esend, erecv, dsend, drecv, psend, precv,
):
    me = Place()
    bar, expected = greet(me)

    def raw(x):
        return lambda b: x[:, :, b * 128 : b * 128 + 128].reshape(TOK, 128).astype(F32)

    for p in range(TC):
        live = (db[0, me.tc, p] >= 0) | (me.tc == p)
        sm[pl.ds(p, 1), :] = jnp.full((1, TOK), jnp.where(live, 0.0, BIG), F32)
    to_heads(raw(k), flip, sk)
    pieces[...] = jnp.zeros(pieces.shape, F32)
    pl.semaphore_wait(bar, expected)
    halo_start(me, c, hrow, hcol, hdiag, hsend, hrecv)
    r_mine = me.x % 2

    def dest(h):
        dev = (NX * me.z + h // NY, 2 * (h % NY) + me.x // 2)
        return dev, (dev[0] == me.tr) & (dev[1] == me.tc)

    def head_copies(act, n, src, dst):
        for h in range(HEADS):
            dev, is_self = dest(h)
            act(is_self, src.at[h], dst.at[r_mine, me.tc], asend.at[n, h], arecv.at[n, r_mine], dev)

    def mask_copies(act):
        for h in range(HEADS):
            dev, is_self = dest(h)
            act(is_self, sm, hm.at[r_mine, me.tc], msend.at[h], mrecv, dev)

    own_k = hk.at[pl.ds(1, 2)]
    own_v = hv.at[pl.ds(1, 2)]
    head_copies(start_or_local, 0, sk, own_k)
    mask_copies(start_or_local)
    to_heads(raw(q), flip, sq)
    head_copies(start_or_local, 1, sq, hq)
    halo_wait(me, c, hrow, hcol, hdiag, hsend, hrecv)
    fill_ext(me, cext, c, hrow, hcol, hdiag)

    def v_block(b):
        lanes = slice(b * 128, b * 128 + 128)
        total = v[:, :, lanes].astype(F32)
        for a in range(3):
            for s in range(3):
                total = total + w[a, s, lanes][None, None, :] * cext[a : a + 2, 7 + s : 71 + s, lanes]
        return total.astype(BF16).astype(F32).reshape(TOK, 128)

    to_heads(v_block, flip, sv)
    head_copies(start_or_local, 2, sv, own_v)
    to_heads(raw(g), flip, sg)
    head_copies(start_or_local, 3, sg, hg)

    def row_copy(at, arr, buf, step):
        src, dst = (buf.at[1], buf.at[3]) if step < 0 else (buf.at[2], buf.at[0])
        return remote(src, dst, bsend.at[arr, at], brecv.at[arr, at], me.chain(step))

    def flip_row(src, out, a):
        def one(j, _):
            out[a, j] = src[a, j].astype(F32).T.astype(BF16)
            return 0

        lax.fori_loop(0, TC, one, 0)

    for n, arr, buf, out in ((0, 0, hk, kt), (2, 1, hv, vt)):
        for at, step in enumerate((-1, 1)):
            wait_bytes(buf.at[1 + at], arecv.at[n, at])

            @pl.when(me.has_chain(step))
            def _():
                row_copy(at, arr, buf, step).start()

        @pl.when(jnp.logical_not(me.has_chain(-1)))
        def _():
            buf[0] = jnp.zeros(buf.shape[1:], BF16)

        @pl.when(jnp.logical_not(me.has_chain(1)))
        def _():
            buf[3] = jnp.zeros(buf.shape[1:], BF16)

        for a in (1, 2):
            flip_row(buf, out, a)
    for n, buf in ((1, hq), (3, hg)):
        for at in range(2):
            wait_bytes(buf.at[at], arecv.at[n, at])
    wait_bytes(hm, mrecv)

    head = me.x * NY + me.y
    acc_k[...] = jnp.zeros(acc_k.shape, F32)
    acc_v[...] = jnp.zeros(acc_v.shape, F32)

    def tile_copy(act, n, src, land, r, j):
        dev = (NX * me.z + 2 * me.c + r, j)
        is_self = (dev[0] == me.tr) & (me.tc == j)
        act(is_self, src.at[r, j], land.at[head], dsend.at[n, r, j], drecv.at[n], dev)

    def edge_copy(arr, r, pair, step):
        view = pl.ds(2 * pair, 2)
        return remote(
            edge.at[arr, r, view], elan.at[arr, 1 - r, view],
            esend.at[arr, r, pair], erecv.at[arr, r], me.chain(step),
        )

    def visit(r, pair):
        j = 2 * pair
        step = 2 * r - 1
        qs = [hq[r, j], hq[r, j + 1]]
        gs = [hg[r, j], hg[r, j + 1]]
        q2 = jnp.concatenate(qs, axis=1)
        g2 = jnp.concatenate(gs, axis=1)
        bias = []
        for p in range(TC):
            bias.append(jnp.concatenate([hm[r, j, pl.ds(p, 1), :], hm[r, j + 1, pl.ds(p, 1), :]], axis=1))
        outer = jnp.full((1, 2 * TOK), jnp.where(me.has_chain(step), 0.0, BIG), F32)
        inner = jnp.zeros((1, 2 * TOK), F32)
        bias.extend([outer, inner] if r == 0 else [inner, outer])
        top = jnp.full((8, 2 * TOK), -3.0e38, F32)
        for p in range(TC + 2):
            if p < TC:
                s = dot(kt[1 + r, p], q2, 1, 0)
            else:
                a = r + 2 * (p - TC)
                s = jnp.concatenate([dot(kt[a, j + t], qs[t], 1, 0) for t in range(2)], axis=1)
            s_buf[p] = s
            top = jnp.maximum(top, jnp.max(s.reshape(TOK // 8, 8, 2 * TOK), axis=0) - bias[p])
        top = jnp.max(top, axis=0, keepdims=True) * EXP_SCALE
        total = jnp.zeros((8, 2 * TOK), F32)
        delta = jnp.zeros((8, 2 * TOK), F32)
        for p in range(TC + 2):
            e = jnp.exp2(s_buf[p] * EXP_SCALE - (top + bias[p]))
            if p < TC:
                gw = dot(vt[1 + r, p], g2, 1, 0)
            else:
                a = r + 2 * (p - TC)
                gw = jnp.concatenate([dot(vt[a, j + t], gs[t], 1, 0) for t in range(2)], axis=1)
            te = e * gw
            s_buf[p] = e
            t_buf[p] = te
            total = total + jnp.sum(e.reshape(TOK // 8, 8, 2 * TOK), axis=0)
            delta = delta + jnp.sum(te.reshape(TOK // 8, 8, 2 * TOK), axis=0)
        inv = 1.0 / jnp.sum(total, axis=0, keepdims=True)
        delta = jnp.sum(delta, axis=0, keepdims=True) * inv
        qn = (q2.astype(F32) * (inv * ROOT)).astype(BF16)
        gn = (g2.astype(F32) * inv).astype(BF16)
        dq = jnp.zeros((PAD_DIM, 2 * TOK), F32)
        for p in range(TC + 2):
            e = s_buf[p]
            ds = (t_buf[p] - e * delta).astype(BF16)
            eb = e.astype(BF16)
            if p < TC:
                dq = dq + dot(hk[1 + r, p], ds, 1, 0)
                acc_k[r, p] += dot(qn, ds, 1, 1)
                acc_v[r, p] += dot(gn, eb, 1, 1)
            else:
                a = r + 2 * (p - TC)
                parts = []
                for t in range(2):
                    half = slice(t * TOK, (t + 1) * TOK)
                    parts.append(dot(hk[a, j + t], ds[:, half], 1, 0))
                    key_term = dot(qn[:, half], ds[:, half], 1, 1)
                    value_term = dot(gn[:, half], eb[:, half], 1, 1)
                    if a in (0, 3):
                        edge[0, r, j + t] = key_term.astype(BF16)
                        edge[1, r, j + t] = value_term.astype(BF16)
                    else:
                        acc_k[1 - r, j + t] += key_term
                        acc_v[1 - r, j + t] += value_term
                dq = dq + jnp.concatenate(parts, axis=1)
        dq = (dq * (inv * ROOT)).astype(BF16)
        tq[r, j] = dq[:, :TOK]
        tq[r, j + 1] = dq[:, TOK:]

        @pl.when(me.has_chain(step))
        def _():
            edge_copy(1, r, pair, step).start()
            edge_copy(0, r, pair, step).start()

        for t in range(2):
            tile_copy(start_or_local, 0, tq, lq, r, j + t)

    for r, step in enumerate((-1, 1)):
        for arr, buf in ((0, hk), (1, hv)):

            @pl.when(me.has_chain(step))
            def _():
                row_copy(1 - r, arr, buf, -step).wait_recv()

        flip_row(hk, kt, 3 * r)
        flip_row(hv, vt, 3 * r)

        def body(pair, _):
            visit(r, pair)
            return 0

        lax.fori_loop(0, TC // 2, body, 0)

    for r, step in ((1, 1), (0, -1)):
        for arr, n, acc, out, land in ((1, 2, acc_v, tv, lv), (0, 1, acc_k, tk, lk)):

            @pl.when(me.has_chain(step))
            def _():
                wait_bytes(elan.at[arr, r], erecv.at[arr, 1 - r])

            extra = jnp.where(me.has_chain(step), elan[arr, r].astype(F32), 0.0)
            out[r] = (acc[r] + extra).astype(BF16)
            for j in range(TC):
                tile_copy(start_or_local, n, out, land, r, j)

    def out_block(out):
        def put(b, x):
            out[:, :, b * 128 : b * 128 + 128] = x.reshape(2, 64, 128).astype(BF16)

        return put

    wait_bytes(lq, drecv.at[0])
    from_heads(lq, flip, out_block(oq))
    wait_bytes(lv, drecv.at[2])
    from_heads(lv, flip, out_block(ov))
    halo_start(me, ov, grow, gcol, gdiag, gsend, grecv)
    for b in range(LANES):
        lanes = slice(b * 128, b * 128 + 128)
        gv = ov[:, :, lanes].astype(F32)
        for a in range(3):
            for s in range(3):
                prod = gv * cext[a : a + 2, 7 + s : 71 + s, lanes]
                t = (a * 3 + s) * LANES + b
                pieces[t // 11, pl.ds(t % 11, 1), :] = jnp.sum(prod.reshape(TOK, 128), axis=0, keepdims=True)

    def exchange(stage, count, mine, src, land, dev):
        def run(act):
            for other in range(count):
                view = src.at[other] if stage == 0 else src
                act(mine == other, view, land.at[mine], psend.at[stage, other], precv.at[stage], dev(other))

        run(start_or_local)
        return run

    runs = []
    runs.append(exchange(0, TC, me.tc, pieces, red1, lambda o: (me.tr, o)))
    wait_bytes(lk, drecv.at[1])
    from_heads(lk, flip, out_block(ok))
    wait_bytes(red1, precv.at[0])
    part2[...] = jnp.sum(red1[...], axis=0)
    runs.append(exchange(1, NX, me.x, part2, red2, lambda o: (NX * me.z + o, me.tc)))
    halo_wait(me, ov, grow, gcol, gdiag, gsend, grecv)
    fill_ext(me, ext, ov, grow, gcol, gdiag)
    wait_bytes(red2, precv.at[1])
    part3[...] = jnp.sum(red2[...], axis=0)
    runs.append(exchange(2, NZ, me.z, part3, red3, lambda o: (NX * o + me.x, me.tc)))
    for b in range(LANES):
        lanes = slice(b * 128, b * 128 + 128)
        total = jnp.zeros((2, 64, 128), F32)
        for a in range(3):
            for s in range(3):
                total = total + w[a, s, lanes][None, None, :] * ext[2 - a : 4 - a, 9 - s : 73 - s, lanes]
        oc[:, :, lanes] = total.astype(BF16)
    wait_bytes(red3, precv.at[2])
    part4[...] = jnp.sum(red3[...], axis=0)
    runs.append(exchange(3, TC, me.tc, part4, red4, lambda o: (me.tr, o)))

    for n, src, dst in ((0, sk, own_k), (1, sq, hq), (2, sv, own_v), (3, sg, hg)):
        head_copies(wait_sent, n, src, dst)
    mask_copies(wait_sent)
    for at, step in enumerate((-1, 1)):

        @pl.when(me.has_chain(step))
        def _():
            for arr, buf in ((0, hk), (1, hv)):
                row_copy(at, arr, buf, step).wait_send()
                for pair in range(TC // 2):
                    edge_copy(arr, at, pair, step).wait_send()

    for n, src, land in ((0, tq, lq), (1, tk, lk), (2, tv, lv)):
        for r in range(2):
            for j in range(TC):
                tile_copy(wait_sent, n, src, land, r, j)

    wait_bytes(red4, precv.at[3])
    for t in range(9 * LANES):
        tap, b = t // LANES, t % LANES
        ow[tap // 3, pl.ds(tap % 3, 1), b * 128 : b * 128 + 128] = red4[t // 11, pl.ds(t % 11, 1), :]
    for run in runs:
        run(wait_sent)


def copy_kernel(*refs):
    n = len(refs) // 2
    for src, dst in zip(refs[:n], refs[n:]):
        dst[...] = src[...]


def vmem_specs(n):
    return [pl.BlockSpec(memory_space=pltpu.VMEM)] * n


def per_device(query, key, value, control, kernel, grad_out, detail_blocks):
    sem = pltpu.SemaphoreType.DMA
    vm = pltpu.VMEM
    img = jax.ShapeDtypeStruct((2, 64, D), BF16)
    outs = (img, img, img, img, jax.ShapeDtypeStruct((3, 3, D), F32))
    rows = lambda n, t=BF16: vm((n, TC, PAD_DIM, TOK), t)
    tiles = vm((HEADS, PAD_DIM, TOK), BF16)
    halo = [vm((2, 64, D), BF16), vm((2, 2, 16, D), BF16), vm((4, 16, D), BF16)]
    reduced = lambda n: vm((n, 16, TOK), F32)
    results = pl.pallas_call(
        whole_kernel,
        out_shape=outs,
        in_specs=vmem_specs(6) + [pl.BlockSpec(memory_space=pltpu.SMEM)],
        out_specs=tuple(vmem_specs(5)),
        scratch_shapes=[rows(2), rows(2), rows(4), rows(4), vm((2, TC, 8, TOK), F32)]
        + [tiles] * 4
        + [vm((8, TOK), F32), vm((D, TOK), F32), vm((4, 80, D), F32), vm((4, 80, D), F32)]
        + halo
        + halo
        + [vm((4, TC, TOK, PAD_DIM), BF16)] * 2
        + [vm((TC + 2, TOK, 2 * TOK), F32)] * 2
        + [rows(2, F32)] * 2
        + [rows(2)] * 3
        + [vm((2, 2, TC, PAD_DIM, TOK), BF16)] * 2
        + [tiles] * 3
        + [reduced(TC), reduced(TC), reduced(NX), reduced(NZ), reduced(TC)]
        + [vm((16, TOK), F32)] * 3
        + [sem((4, HEADS)), sem((4, 2)), sem((HEADS,)), sem, sem((2, 2)), sem((2, 2))]
        + [sem((8,))] * 4
        + [sem((2, 2, 4)), sem((2, 2)), sem((3, 2, TC)), sem((3,)), sem((4, 8)), sem((4,))],
        compiler_params=pltpu.CompilerParams(collective_id=0, has_side_effects=True),
        name="whole",
    )(query, key, value, grad_out, control, kernel, detail_blocks)
    return pl.pallas_call(
        copy_kernel,
        out_shape=outs,
        in_specs=vmem_specs(5),
        out_specs=tuple(vmem_specs(5)),
        name="finish",
    )(*results)


def solution(mesh):
    tile = P("trow", "tcol", None)
    return jax.shard_map(
        per_device,
        mesh=mesh,
        in_specs=(tile, tile, tile, tile, P(), tile, P("trow", None, None)),
        out_specs=(tile, tile, tile, tile, P()),
        check_vma=False,
    )
```

```python
import functools
import math

import jax
import jax.numpy as jnp
from jax import lax
from jax.experimental import pallas as pl
from jax.experimental.pallas import tpu as pltpu
from jax.sharding import PartitionSpec as P

HEADS = 16
HEAD_DIM = 72
PAD_DIM = 80
D = 1152
TOK = 128
NX = 4
NY = 4
TR = 32
TC = 8
NZ = TR // NX
LANES = D // 128
ROOT = HEAD_DIM ** (-0.5)
EXP_SCALE = ROOT * math.log2(math.e)
BIG = 1e30
MESH = pl.DeviceIdType.MESH
F32 = jnp.float32
BF16 = jnp.bfloat16
DIRS = ((-1, -1), (-1, 0), (-1, 1), (0, -1), (0, 1), (1, -1), (1, 0), (1, 1))


class Place:
    def __init__(self):
        self.tr = lax.axis_index("trow")
        self.tc = lax.axis_index("tcol")
        self.z = self.tr // NX
        self.x = self.tr % NX
        self.y = self.tc // 2
        self.c = self.tc % 2
        self.u = 2 * self.z + self.c

    def chain(self, step):
        u = self.u + step
        return (NX * (u // 2) + self.x, 2 * self.y + u % 2)

    def has_chain(self, step):
        u = self.u + step
        return (u >= 0) & (u < 2 * NZ)

    def has_dir(self, dr, dc):
        r = self.tr + dr
        c = self.tc + dc
        return (r >= 0) & (r < TR) & (c >= 0) & (c < TC)


def signal(sem, dev):
    pl.semaphore_signal(sem, inc=1, device_id=dev, device_id_type=MESH)


def greet(me):
    bar = pltpu.get_barrier_semaphore()
    total = jnp.int32(NX * TC - 1)
    for step in range(1, NX * TC):
        rank = (me.x * TC + me.tc + step) % (NX * TC)
        signal(bar, (NX * me.z + rank // TC, rank % TC))
    for step in (-1, 1):
        ok = me.has_chain(step)
        total = total + ok.astype(jnp.int32)

        @pl.when(ok)
        def _():
            signal(bar, me.chain(step))

    for dr, dc in DIRS:
        ok = me.has_dir(dr, dc)
        total = total + ok.astype(jnp.int32)

        @pl.when(ok)
        def _():
            signal(bar, (me.tr + dr, me.tc + dc))

    for step in range(1, NZ):
        signal(bar, (NX * ((me.z + step) % NZ) + me.x, me.tc))
    return bar, total + (NZ - 1)


def remote(src, dst, ssem, rsem, dev):
    return pltpu.make_async_remote_copy(
        src_ref=src, dst_ref=dst, send_sem=ssem, recv_sem=rsem, device_id=dev, device_id_type=MESH
    )


def start_or_local(is_self, src, dst, ssem, rsem, dev):
    @pl.when(is_self)
    def _():
        pltpu.make_async_copy(src, dst, rsem).start()

    @pl.when(jnp.logical_not(is_self))
    def _():
        remote(src, dst, ssem, rsem, dev).start()


def wait_sent(is_self, src, dst, ssem, rsem, dev):
    @pl.when(jnp.logical_not(is_self))
    def _():
        remote(src, dst, ssem, rsem, dev).wait_send()


def wait_bytes(ref, sem):
    pltpu.make_async_copy(ref, ref, sem).wait()


def pack_rim(img, pack):
    for side in range(2):
        for r in range(2):
            for b in range(LANES):
                block = img[r, 48 * side : 48 * side + 16, b * 128 : b * 128 + 128].astype(F32)
                pack[side, r, b : b + 1, :] = block[15 * side : 15 * side + 1]


def halo_views(img, pack, rows, cols, diag, dr, dc):
    row = 0 if dr < 0 else 1
    side = 0 if dc < 0 else 1
    if dc == 0:
        return img.at[row], rows.at[1 if dr < 0 else 0]
    if dr == 0:
        return pack.at[side], cols.at[1 - side]
    return pack.at[side, row], diag.at[(2 if dr < 0 else 0) + 1 - side]


def halo_start(me, img, pack, rows, cols, diag, ssem, rsem):
    for at, (dr, dc) in enumerate(DIRS):
        src, dst = halo_views(img, pack, rows, cols, diag, dr, dc)

        @pl.when(me.has_dir(dr, dc))
        def _():
            remote(src, dst, ssem.at[at], rsem.at[at], (me.tr + dr, me.tc + dc)).start()


def halo_wait(me, img, pack, rows, cols, diag, ssem, rsem):
    for at, (dr, dc) in enumerate(DIRS):
        src, dst = halo_views(img, pack, rows, cols, diag, dr, dc)

        @pl.when(me.has_dir(dr, dc))
        def _():
            remote(src, dst, ssem.at[at], rsem.at[at], (me.tr + dr, me.tc + dc)).wait_send()

        @pl.when(me.has_dir(-dr, -dc))
        def _():
            remote(src, dst, ssem.at[at], rsem.at[at], (me.tr - dr, me.tc - dc)).wait_recv()


def fill_ext(me, ext, img, rows, cols, diag):
    ext[1:3, 8:72, :] = img[...].astype(F32)
    up = me.has_dir(-1, 0)
    down = me.has_dir(1, 0)
    left = me.has_dir(0, -1)
    right = me.has_dir(0, 1)

    def put(ok, place, value):
        ext[place] = jnp.where(ok, value.astype(F32), 0.0)

    put(up, (0, slice(8, 72)), rows[0])
    put(down, (3, slice(8, 72)), rows[1])
    for b in range(LANES):
        lanes = slice(b * 128, b * 128 + 128)
        piece = slice(b, b + 1)
        for r in range(2):
            put(left, (1 + r, slice(7, 8), lanes), cols[0, r, piece])
            put(right, (1 + r, slice(72, 73), lanes), cols[1, r, piece])
        put(up & left, (0, slice(7, 8), lanes), diag[0, piece])
        put(up & right, (0, slice(72, 73), lanes), diag[1, piece])
        put(down & left, (3, slice(7, 8), lanes), diag[2, piece])
        put(down & right, (3, slice(72, 73), lanes), diag[3, piece])


def to_heads(x, flip, out, tail=None):
    for b in range(LANES):
        flip[pl.ds(b * 128, 128), :] = x(b).T
    if tail is None:
        tail = jnp.zeros((PAD_DIM - HEAD_DIM, TOK), F32)
    for h in range(HEADS):
        out[h] = jnp.concatenate([flip[pl.ds(h * HEAD_DIM, HEAD_DIM), :], tail], axis=0).astype(BF16)


def dot(a, b, ca, cb):
    return lax.dot_general(a, b, (((ca,), (cb,)), ((), ())), preferred_element_type=F32)


def from_heads(land, flip, put):
    for h in range(HEADS):
        flip[pl.ds(h * HEAD_DIM, HEAD_DIM), :] = land[h].astype(F32)[:HEAD_DIM]
    for b in range(LANES):
        put(b, flip[pl.ds(b * 128, 128), :].T)


def whole_kernel(
    q_hbm, k_hbm, v_hbm, g_hbm, c_hbm, w, db,
    oq, ok, ov, oc, ow,
    q, k, v, g, c,
    hq, hg, hk, hv,
    sq, sg, sk, sv, flip, ext, cext, cpack, hrow, hcol, hdiag, gpack, grow, gcol, gdiag,
    kt, vt, s_buf, g_buf, e_buf, d_buf, top_buf, inv_buf, qn_buf, gn_buf,
    acc_k, acc_v, tq, tk, tv, edge, elan, lq, lk, lv,
    pieces, red1, red2, red3, red4, part2, part3, part4,
    isem, asend, arecv, bsend, brecv, hsend, hrecv, gsend, grecv,
    esend, erecv, dsend, drecv, psend, precv,
):
    me = Place()
    loads = [
        pltpu.make_async_copy(src, dst, isem.at[at])
        for at, (src, dst) in enumerate(((k_hbm, k), (c_hbm, c), (q_hbm, q), (v_hbm, v), (g_hbm, g)))
    ]
    for load in loads:
        load.start()
    bar, expected = greet(me)

    def raw(x):
        return lambda b: x[:, :, b * 128 : b * 128 + 128].reshape(TOK, 128).astype(F32)

    loads[0].wait()
    to_heads(raw(k), flip, sk)
    loads[1].wait()
    pack_rim(c, cpack)
    pieces[...] = jnp.zeros(pieces.shape, F32)
    pl.semaphore_wait(bar, expected)
    halo_start(me, c, cpack, hrow, hcol, hdiag, hsend, hrecv)
    r_mine = me.x % 2

    def dest(h):
        dev = (NX * me.z + h // NY, 2 * (h % NY) + me.x // 2)
        return dev, (dev[0] == me.tr) & (dev[1] == me.tc)

    def head_copies(act, n, src, dst):
        for h in range(HEADS):
            dev, is_self = dest(h)
            act(is_self, src.at[h], dst.at[r_mine, me.tc], asend.at[n, h], arecv.at[n, r_mine], dev)

    own_k = hk.at[pl.ds(1, 2)]
    own_v = hv.at[pl.ds(1, 2)]
    head_copies(start_or_local, 0, sk, own_k)
    loads[2].wait()
    row_id = lax.broadcasted_iota(jnp.int32, (TC, TOK), 0)
    dead = jnp.zeros((TC, TOK), F32)
    for p in range(TC):
        live = (db[0, me.tc, p] >= 0) | (me.tc == p)
        dead = jnp.where(row_id == p, jnp.where(live, 0.0, BIG), dead)
    to_heads(raw(q), flip, sq, dead)
    head_copies(start_or_local, 1, sq, hq)
    halo_wait(me, c, cpack, hrow, hcol, hdiag, hsend, hrecv)
    fill_ext(me, cext, c, hrow, hcol, hdiag)

    loads[3].wait()

    def v_block(b):
        lanes = slice(b * 128, b * 128 + 128)
        total = v[:, :, lanes].astype(F32)
        for a in range(3):
            for s in range(3):
                total = total + w[a, s, lanes][None, None, :] * cext[a : a + 2, 7 + s : 71 + s, lanes]
        return total.astype(BF16).astype(F32).reshape(TOK, 128)

    to_heads(v_block, flip, sv)
    head_copies(start_or_local, 2, sv, own_v)
    loads[4].wait()
    to_heads(raw(g), flip, sg)
    head_copies(start_or_local, 3, sg, hg)

    def row_copy(at, arr, buf, step):
        src, dst = (buf.at[1], buf.at[3]) if step < 0 else (buf.at[2], buf.at[0])
        return remote(src, dst, bsend.at[arr, at], brecv.at[arr, at], me.chain(step))

    def flip_row(src, out, a):
        for j in range(TC):
            out[a, j] = src[a, j].astype(F32).T.astype(BF16)

    for n, arr, buf, out in ((0, 0, hk, kt), (2, 1, hv, vt)):
        for at, step in enumerate((-1, 1)):
            wait_bytes(buf.at[1 + at], arecv.at[n, at])

            @pl.when(me.has_chain(step))
            def _():
                row_copy(at, arr, buf, step).start()

        @pl.when(jnp.logical_not(me.has_chain(-1)))
        def _():
            buf[0] = jnp.zeros(buf.shape[1:], BF16)

        @pl.when(jnp.logical_not(me.has_chain(1)))
        def _():
            buf[3] = jnp.zeros(buf.shape[1:], BF16)

        for a in (1, 2):
            flip_row(buf, out, a)
    for n, buf in ((1, hq), (3, hg)):
        for at in range(2):
            wait_bytes(buf.at[at], arecv.at[n, at])

    head = me.x * NY + me.y

    def tile_copy(act, n, src, land, r, j):
        dev = (NX * me.z + 2 * me.c + r, j)
        is_self = (dev[0] == me.tr) & (me.tc == j)
        act(is_self, src.at[r, j], land.at[head], dsend.at[n, r, j], drecv.at[n], dev)

    def edge_copy(arr, r, pair, step):
        view = pl.ds(2 * pair, 2)
        return remote(
            edge.at[arr, r, view], elan.at[arr, 1 - r, view],
            esend.at[arr, r, pair], erecv.at[arr, r], me.chain(step),
        )

    def halves(t):
        return slice(t * TOK, (t + 1) * TOK)

    def scores(i):
        r, j, par = i // 4, 2 * (i % 4), i % 2
        qs = [hq[r, j], hq[r, j + 1]]
        gs = [hg[r, j], hg[r, j + 1]]
        q2 = jnp.concatenate(qs, axis=1)
        g2 = jnp.concatenate(gs, axis=1)
        dead = q2[HEAD_DIM:].astype(F32)
        far = jnp.where(me.has_chain(2 * r - 1), 0.0, BIG)
        top = jnp.full((8, 2 * TOK), -3.0e38, F32)
        for p in range(TC + 2):
            if p < TC:
                s_buf[par, p] = dot(kt[1 + r, p], q2, 1, 0)
                g_buf[par, p] = dot(vt[1 + r, p], g2, 1, 0)
                bias = dead[p : p + 1]
            else:
                a = r + 2 * (p - TC)
                for t in range(2):
                    s_buf[par, p, :, halves(t)] = dot(kt[a, j + t], qs[t], 1, 0)
                    g_buf[par, p, :, halves(t)] = dot(vt[a, j + t], gs[t], 1, 0)
                bias = far if a in (0, 3) else 0.0
            top = jnp.maximum(top, jnp.max(s_buf[par, p].reshape(TOK // 8, 8, 2 * TOK), axis=0) - bias)
        top_buf[par] = top

    def soften(i):
        r, j, par = i // 4, 2 * (i % 4), i % 2
        q2 = jnp.concatenate([hq[r, j], hq[r, j + 1]], axis=1).astype(F32)
        g2 = jnp.concatenate([hg[r, j], hg[r, j + 1]], axis=1).astype(F32)
        dead = q2[HEAD_DIM:]
        far = jnp.where(me.has_chain(2 * r - 1), 0.0, BIG)
        top = jnp.max(top_buf[par], axis=0, keepdims=True) * EXP_SCALE
        total = jnp.zeros((8, 2 * TOK), F32)
        delta = jnp.zeros((8, 2 * TOK), F32)
        for p in range(TC + 2):
            if p < TC:
                shift = top + dead[p : p + 1]
            else:
                shift = top + far if r + 2 * (p - TC) in (0, 3) else top
            e = jnp.exp2(s_buf[par, p] * EXP_SCALE - shift)
            s_buf[par, p] = e
            e_buf[par, p] = e.astype(BF16)
            total = total + jnp.sum(e.reshape(TOK // 8, 8, 2 * TOK), axis=0)
            delta = delta + jnp.sum((e * g_buf[par, p]).reshape(TOK // 8, 8, 2 * TOK), axis=0)
        inv = 1.0 / jnp.sum(total, axis=0, keepdims=True)
        delta = jnp.sum(delta, axis=0, keepdims=True) * inv
        for p in range(TC + 2):
            d_buf[par, p] = (s_buf[par, p] * (g_buf[par, p] - delta)).astype(BF16)
        scaled = inv * ROOT
        inv_buf[par] = jnp.broadcast_to(scaled, (8, 2 * TOK))
        qn_buf[par] = (q2 * scaled).astype(BF16)
        gn_buf[par] = (g2 * inv).astype(BF16)

    def grads(i):
        r, j, par = i // 4, 2 * (i % 4), i % 2
        qn = qn_buf[par]
        gn = gn_buf[par]

        def add(acc, at, tile, value, first):
            acc[at, tile] = value if first else acc[at, tile] + value

        ds_row = jnp.concatenate([d_buf[par, p] for p in range(TC)], axis=0)
        e_row = jnp.concatenate([e_buf[par, p] for p in range(TC)], axis=0)
        dq = dot(jnp.concatenate([hk[1 + r, p] for p in range(TC)], axis=1), ds_row, 1, 0)
        key_row = dot(qn, ds_row, 1, 1)
        value_row = dot(gn, e_row, 1, 1)
        for p in range(TC):
            add(acc_k, r, p, key_row[:, halves(p)], i == 0)
            add(acc_v, r, p, value_row[:, halves(p)], i == 0)
        parts = []
        for t in range(2):
            part = jnp.zeros((PAD_DIM, TOK), F32)
            for p in range(TC, TC + 2):
                a = r + 2 * (p - TC)
                ds = d_buf[par, p, :, halves(t)]
                part = part + dot(hk[a, j + t], ds, 1, 0)
                key_term = dot(qn[:, halves(t)], ds, 1, 1)
                value_term = dot(gn[:, halves(t)], e_buf[par, p, :, halves(t)], 1, 1)
                if a in (0, 3):
                    edge[0, r, j + t] = key_term.astype(BF16)
                    edge[1, r, j + t] = value_term.astype(BF16)
                else:
                    add(acc_k, 1 - r, j + t, key_term, r == 0)
                    add(acc_v, 1 - r, j + t, value_term, r == 0)
            parts.append(part)
        dq = ((dq + jnp.concatenate(parts, axis=1)) * inv_buf[par, 0:1]).astype(BF16)
        tq[r, j] = dq[:, :TOK]
        tq[r, j + 1] = dq[:, TOK:]

    def send_terms(i):
        r, pair = i // 4, i % 4
        step = 2 * r - 1

        @pl.when(me.has_chain(step))
        def _():
            edge_copy(1, r, pair, step).start()
            edge_copy(0, r, pair, step).start()

        for t in range(2):
            tile_copy(start_or_local, 0, tq, lq, r, 2 * pair + t)

    def take_outer(r):
        step = 2 * r - 1
        for arr, buf in ((0, hk), (1, hv)):

            @pl.when(me.has_chain(step))
            def _():
                row_copy(1 - r, arr, buf, -step).wait_recv()

        flip_row(hk, kt, 3 * r)
        flip_row(hv, vt, 3 * r)

    visits = TC
    take_outer(0)
    scores(0)
    for i in range(visits + 1):
        if i + 1 == visits // 2:
            take_outer(1)
        if i >= 1:
            grads(i - 1)
        if i < visits:
            soften(i)
        if i + 1 < visits:
            scores(i + 1)
        if i >= 1:
            send_terms(i - 1)

    for r, step in ((1, 1), (0, -1)):
        for arr, n, acc, out, land in ((1, 2, acc_v, tv, lv), (0, 1, acc_k, tk, lk)):

            @pl.when(me.has_chain(step))
            def _():
                wait_bytes(elan.at[arr, r], erecv.at[arr, 1 - r])

            extra = jnp.where(me.has_chain(step), elan[arr, r].astype(F32), 0.0)
            for j in range(TC):
                out[r, j] = (acc[r, j] + extra[j]).astype(BF16)
            for j in range(TC):
                tile_copy(start_or_local, n, out, land, r, j)

    def out_block(out):
        def put(b, x):
            out[:, :, b * 128 : b * 128 + 128] = x.reshape(2, 64, 128).astype(BF16)

        return put

    wait_bytes(lq, drecv.at[0])
    from_heads(lq, flip, out_block(oq))
    wait_bytes(lv, drecv.at[2])
    from_heads(lv, flip, out_block(ov))
    pack_rim(ov, gpack)
    halo_start(me, ov, gpack, grow, gcol, gdiag, gsend, grecv)
    for b in range(LANES):
        lanes = slice(b * 128, b * 128 + 128)
        gv = ov[:, :, lanes].astype(F32)
        for a in range(3):
            for s in range(3):
                prod = gv * cext[a : a + 2, 7 + s : 71 + s, lanes]
                t = (a * 3 + s) * LANES + b
                pieces[t // 11, pl.ds(t % 11, 1), :] = jnp.sum(prod.reshape(TOK, 128), axis=0, keepdims=True)

    def exchange(stage, count, mine, src, land, dev):
        def run(act):
            for other in range(count):
                view = src.at[other] if stage == 0 else src
                act(mine == other, view, land.at[mine], psend.at[stage, other], precv.at[stage], dev(other))

        run(start_or_local)
        return run

    runs = []
    runs.append(exchange(0, TC, me.tc, pieces, red1, lambda o: (me.tr, o)))
    wait_bytes(lk, drecv.at[1])
    from_heads(lk, flip, out_block(ok))
    wait_bytes(red1, precv.at[0])
    part2[...] = jnp.sum(red1[...], axis=0)
    runs.append(exchange(1, NX, me.x, part2, red2, lambda o: (NX * me.z + o, me.tc)))
    halo_wait(me, ov, gpack, grow, gcol, gdiag, gsend, grecv)
    fill_ext(me, ext, ov, grow, gcol, gdiag)
    wait_bytes(red2, precv.at[1])
    part3[...] = jnp.sum(red2[...], axis=0)
    runs.append(exchange(2, NZ, me.z, part3, red3, lambda o: (NX * o + me.x, me.tc)))
    for b in range(LANES):
        lanes = slice(b * 128, b * 128 + 128)
        total = jnp.zeros((2, 64, 128), F32)
        for a in range(3):
            for s in range(3):
                total = total + w[a, s, lanes][None, None, :] * ext[2 - a : 4 - a, 9 - s : 73 - s, lanes]
        oc[:, :, lanes] = total.astype(BF16)
    wait_bytes(red3, precv.at[2])
    part4[...] = jnp.sum(red3[...], axis=0)
    runs.append(exchange(3, TC, me.tc, part4, red4, lambda o: (me.tr, o)))

    for n, src, dst in ((0, sk, own_k), (1, sq, hq), (2, sv, own_v), (3, sg, hg)):
        head_copies(wait_sent, n, src, dst)
    for at, step in enumerate((-1, 1)):

        @pl.when(me.has_chain(step))
        def _():
            for arr, buf in ((0, hk), (1, hv)):
                row_copy(at, arr, buf, step).wait_send()
                for pair in range(TC // 2):
                    edge_copy(arr, at, pair, step).wait_send()

    for n, src, land in ((0, tq, lq), (1, tk, lk), (2, tv, lv)):
        for r in range(2):
            for j in range(TC):
                tile_copy(wait_sent, n, src, land, r, j)

    wait_bytes(red4, precv.at[3])
    for t in range(9 * LANES):
        tap, b = t // LANES, t % LANES
        ow[tap // 3, pl.ds(tap % 3, 1), b * 128 : b * 128 + 128] = red4[t // 11, pl.ds(t % 11, 1), :]
    for run in runs:
        run(wait_sent)


def copy_kernel(*refs):
    n = len(refs) // 2
    for src, dst in zip(refs[:n], refs[n:]):
        dst[...] = src[...]


def vmem_specs(n):
    return [pl.BlockSpec(memory_space=pltpu.VMEM)] * n


def per_device(query, key, value, control, kernel, grad_out, detail_blocks):
    sem = pltpu.SemaphoreType.DMA
    vm = pltpu.VMEM
    img = jax.ShapeDtypeStruct((2, 64, D), BF16)
    outs = (img, img, img, img, jax.ShapeDtypeStruct((3, 3, D), F32))
    rows = lambda n, t=BF16: vm((n, TC, PAD_DIM, TOK), t)
    tiles = vm((HEADS, PAD_DIM, TOK), BF16)
    halo = [vm((2, 2, 16, TOK), F32), vm((2, 64, D), BF16), vm((2, 2, 16, TOK), F32), vm((4, 16, TOK), F32)]
    pair = lambda t: vm((2, TC + 2, TOK, 2 * TOK), t)
    wide = vm((2, 8, 2 * TOK), F32)
    reduced = lambda n: vm((n, 16, TOK), F32)
    results = pl.pallas_call(
        whole_kernel,
        out_shape=outs,
        in_specs=[pl.BlockSpec(memory_space=pl.ANY)] * 5 + vmem_specs(1) + [pl.BlockSpec(memory_space=pltpu.SMEM)],
        out_specs=tuple(vmem_specs(5)),
        scratch_shapes=[vm((2, 64, D), BF16)] * 5
        + [rows(2), rows(2), rows(4), rows(4)]
        + [tiles] * 4
        + [vm((D, TOK), F32), vm((4, 80, D), F32), vm((4, 80, D), F32)]
        + halo
        + halo
        + [vm((4, TC, TOK, PAD_DIM), BF16)] * 2
        + [pair(F32), pair(F32), pair(BF16), pair(BF16), wide, wide]
        + [vm((2, PAD_DIM, 2 * TOK), BF16)] * 2
        + [rows(2, F32)] * 2
        + [rows(2)] * 3
        + [vm((2, 2, TC, PAD_DIM, TOK), BF16)] * 2
        + [tiles] * 3
        + [reduced(TC), reduced(TC), reduced(NX), reduced(NZ), reduced(TC)]
        + [vm((16, TOK), F32)] * 3
        + [sem((5,)), sem((4, HEADS)), sem((4, 2)), sem((2, 2)), sem((2, 2))]
        + [sem((8,))] * 4
        + [sem((2, 2, 4)), sem((2, 2)), sem((3, 2, TC)), sem((3,)), sem((4, 8)), sem((4,))],
        compiler_params=pltpu.CompilerParams(collective_id=0, has_side_effects=True),
        name="whole",
    )(query, key, value, grad_out, control, kernel, detail_blocks)
    return pl.pallas_call(
        copy_kernel,
        out_shape=outs,
        in_specs=vmem_specs(5),
        out_specs=tuple(vmem_specs(5)),
        name="finish",
    )(*results)


def solution(mesh):
    tile = P("trow", "tcol", None)
    return jax.shard_map(
        per_device,
        mesh=mesh,
        in_specs=(tile, tile, tile, tile, P(), tile, P("trow", None, None)),
        out_specs=(tile, tile, tile, tile, P()),
        check_vma=False,
    )
```

```python
import functools
import math

import jax
import jax.numpy as jnp
from jax import lax
from jax.experimental import pallas as pl
from jax.experimental.pallas import tpu as pltpu
from jax.sharding import PartitionSpec as P

HEADS = 16
HEAD_DIM = 72
PAD_DIM = 80
D = 1152
TOK = 128
NX = 4
NY = 4
TR = 32
TC = 8
NZ = TR // NX
LANES = D // 128
ROOT = HEAD_DIM ** (-0.5)
EXP_SCALE = ROOT * math.log2(math.e)
BIG = 1e30
MESH = pl.DeviceIdType.MESH
F32 = jnp.float32
BF16 = jnp.bfloat16
DIRS = ((-1, -1), (-1, 0), (-1, 1), (0, -1), (0, 1), (1, -1), (1, 0), (1, 1))


class Place:
    def __init__(self):
        self.tr = lax.axis_index("trow")
        self.tc = lax.axis_index("tcol")
        self.z = self.tr // NX
        self.x = self.tr % NX
        self.y = self.tc // 2
        self.c = self.tc % 2
        self.u = 2 * self.z + self.c

    def chain(self, step):
        u = self.u + step
        return (NX * (u // 2) + self.x, 2 * self.y + u % 2)

    def has_chain(self, step):
        u = self.u + step
        return (u >= 0) & (u < 2 * NZ)

    def has_dir(self, dr, dc):
        r = self.tr + dr
        c = self.tc + dc
        return (r >= 0) & (r < TR) & (c >= 0) & (c < TC)


def signal(sem, dev):
    pl.semaphore_signal(sem, inc=1, device_id=dev, device_id_type=MESH)


def greet(me):
    bar = pltpu.get_barrier_semaphore()
    total = jnp.int32(NX * TC - 1)
    for step in range(1, NX * TC):
        rank = (me.x * TC + me.tc + step) % (NX * TC)
        signal(bar, (NX * me.z + rank // TC, rank % TC))
    for step in (-1, 1):
        ok = me.has_chain(step)
        total = total + ok.astype(jnp.int32)

        @pl.when(ok)
        def _():
            signal(bar, me.chain(step))

    for dr, dc in DIRS:
        ok = me.has_dir(dr, dc)
        total = total + ok.astype(jnp.int32)

        @pl.when(ok)
        def _():
            signal(bar, (me.tr + dr, me.tc + dc))

    for step in range(1, NZ):
        signal(bar, (NX * ((me.z + step) % NZ) + me.x, me.tc))
    return bar, total + (NZ - 1)


def remote(src, dst, ssem, rsem, dev):
    return pltpu.make_async_remote_copy(
        src_ref=src, dst_ref=dst, send_sem=ssem, recv_sem=rsem, device_id=dev, device_id_type=MESH
    )


def start_or_local(is_self, src, dst, ssem, rsem, dev):
    @pl.when(is_self)
    def _():
        pltpu.make_async_copy(src, dst, rsem).start()

    @pl.when(jnp.logical_not(is_self))
    def _():
        remote(src, dst, ssem, rsem, dev).start()


def wait_sent(is_self, src, dst, ssem, rsem, dev):
    @pl.when(jnp.logical_not(is_self))
    def _():
        remote(src, dst, ssem, rsem, dev).wait_send()


def wait_bytes(ref, sem):
    pltpu.make_async_copy(ref, ref, sem).wait()


def pack_rim(img, pack):
    for side in range(2):
        for r in range(2):
            for b in range(LANES):
                block = img[r, 48 * side : 48 * side + 16, b * 128 : b * 128 + 128].astype(F32)
                pack[side, r, b : b + 1, :] = block[15 * side : 15 * side + 1]


def halo_views(img, pack, rows, cols, diag, dr, dc):
    row = 0 if dr < 0 else 1
    side = 0 if dc < 0 else 1
    if dc == 0:
        return img.at[row], rows.at[1 if dr < 0 else 0]
    if dr == 0:
        return pack.at[side], cols.at[1 - side]
    return pack.at[side, row], diag.at[(2 if dr < 0 else 0) + 1 - side]


def halo_start(me, img, pack, rows, cols, diag, ssem, rsem):
    for at, (dr, dc) in enumerate(DIRS):
        src, dst = halo_views(img, pack, rows, cols, diag, dr, dc)

        @pl.when(me.has_dir(dr, dc))
        def _():
            remote(src, dst, ssem.at[at], rsem.at[at], (me.tr + dr, me.tc + dc)).start()


def halo_wait(me, img, pack, rows, cols, diag, ssem, rsem):
    for at, (dr, dc) in enumerate(DIRS):
        src, dst = halo_views(img, pack, rows, cols, diag, dr, dc)

        @pl.when(me.has_dir(dr, dc))
        def _():
            remote(src, dst, ssem.at[at], rsem.at[at], (me.tr + dr, me.tc + dc)).wait_send()

        @pl.when(me.has_dir(-dr, -dc))
        def _():
            remote(src, dst, ssem.at[at], rsem.at[at], (me.tr - dr, me.tc - dc)).wait_recv()


def fill_ext(me, ext, img, rows, cols, diag):
    ext[1:3, 8:72, :] = img[...].astype(F32)
    up = me.has_dir(-1, 0)
    down = me.has_dir(1, 0)
    left = me.has_dir(0, -1)
    right = me.has_dir(0, 1)

    def put(ok, place, value):
        ext[place] = jnp.where(ok, value.astype(F32), 0.0)

    put(up, (0, slice(8, 72)), rows[0])
    put(down, (3, slice(8, 72)), rows[1])
    for b in range(LANES):
        lanes = slice(b * 128, b * 128 + 128)
        piece = slice(b, b + 1)
        for r in range(2):
            put(left, (1 + r, slice(7, 8), lanes), cols[0, r, piece])
            put(right, (1 + r, slice(72, 73), lanes), cols[1, r, piece])
        put(up & left, (0, slice(7, 8), lanes), diag[0, piece])
        put(up & right, (0, slice(72, 73), lanes), diag[1, piece])
        put(down & left, (3, slice(7, 8), lanes), diag[2, piece])
        put(down & right, (3, slice(72, 73), lanes), diag[3, piece])


def to_heads(x, flip, out, tail=None):
    for b in range(LANES):
        flip[pl.ds(b * 128, 128), :] = x(b).T
    if tail is None:
        tail = jnp.zeros((PAD_DIM - HEAD_DIM, TOK), F32)
    for h in range(HEADS):
        out[h] = jnp.concatenate([flip[pl.ds(h * HEAD_DIM, HEAD_DIM), :], tail], axis=0).astype(BF16)


def dot(a, b, ca, cb):
    return lax.dot_general(a, b, (((ca,), (cb,)), ((), ())), preferred_element_type=F32)


def from_heads(land, flip, put):
    for h in range(HEADS):
        flip[pl.ds(h * HEAD_DIM, HEAD_DIM), :] = land[h].astype(F32)[:HEAD_DIM]
    for b in range(LANES):
        put(b, flip[pl.ds(b * 128, 128), :].T)


def whole_kernel(
    q_hbm, k_hbm, v_hbm, g_hbm, c_hbm, w, db,
    oq, ok, ov, oc, ow,
    q, k, v, g, c,
    hq, hg, hk, hv, hc,
    sq, sg, sk, sv, sc, flip, ext, cext, cpack, hrow, hcol, hdiag, gpack, grow, gcol, gdiag,
    kt, vt, s_buf, g_buf, e_buf, d_buf, top_buf, inv_buf, qn_buf, gn_buf,
    acc_k, acc_v, tq, tk, tv, edge, elan, lq, lk, lv,
    taps, red1, red2, red3, part1, part2, part3,
    isem, asend, arecv, bsend, brecv, hsend, hrecv, gsend, grecv,
    esend, erecv, dsend, drecv, psend, precv,
):
    me = Place()
    loads = [
        pltpu.make_async_copy(src, dst, isem.at[at])
        for at, (src, dst) in enumerate(((k_hbm, k), (c_hbm, c), (q_hbm, q), (v_hbm, v), (g_hbm, g)))
    ]
    for load in loads:
        load.start()
    bar, expected = greet(me)

    def raw(x):
        return lambda b: x[:, :, b * 128 : b * 128 + 128].reshape(TOK, 128).astype(F32)

    loads[0].wait()
    to_heads(raw(k), flip, sk)
    loads[1].wait()
    pack_rim(c, cpack)
    pl.semaphore_wait(bar, expected)
    halo_start(me, c, cpack, hrow, hcol, hdiag, hsend, hrecv)
    r_mine = me.x % 2

    def dest(h):
        dev = (NX * me.z + h // NY, 2 * (h % NY) + me.x // 2)
        return dev, (dev[0] == me.tr) & (dev[1] == me.tc)

    def head_copies(act, n, src, dst):
        for h in range(HEADS):
            dev, is_self = dest(h)
            act(is_self, src.at[h], dst.at[r_mine, me.tc], asend.at[n, h], arecv.at[n, r_mine], dev)

    own_k = hk.at[pl.ds(1, 2)]
    own_v = hv.at[pl.ds(1, 2)]
    head_copies(start_or_local, 0, sk, own_k)
    loads[2].wait()
    row_id = lax.broadcasted_iota(jnp.int32, (TC, TOK), 0)
    dead = jnp.zeros((TC, TOK), F32)
    for p in range(TC):
        live = (db[0, me.tc, p] >= 0) | (me.tc == p)
        dead = jnp.where(row_id == p, jnp.where(live, 0.0, BIG), dead)
    to_heads(raw(q), flip, sq, dead)
    head_copies(start_or_local, 1, sq, hq)
    halo_wait(me, c, cpack, hrow, hcol, hdiag, hsend, hrecv)
    fill_ext(me, cext, c, hrow, hcol, hdiag)

    loads[3].wait()

    def v_block(b):
        lanes = slice(b * 128, b * 128 + 128)
        total = v[:, :, lanes].astype(F32)
        for a in range(3):
            for s in range(3):
                total = total + w[a, s, lanes][None, None, :] * cext[a : a + 2, 7 + s : 71 + s, lanes]
        return total.astype(BF16).astype(F32).reshape(TOK, 128)

    to_heads(v_block, flip, sv)
    head_copies(start_or_local, 2, sv, own_v)
    loads[4].wait()
    to_heads(raw(g), flip, sg)
    head_copies(start_or_local, 3, sg, hg)
    own_c = hc.at[pl.ds(1, 2)]
    to_heads(raw(c), flip, sc)
    head_copies(start_or_local, 4, sc, own_c)

    def row_copy(at, arr, buf, step):
        src, dst = (buf.at[1], buf.at[3]) if step < 0 else (buf.at[2], buf.at[0])
        return remote(src, dst, bsend.at[arr, at], brecv.at[arr, at], me.chain(step))

    def flip_row(src, out, a):
        for j in range(TC):
            out[a, j] = src[a, j].astype(F32).T.astype(BF16)

    def pass_rows(n, arr, buf):
        for at, step in enumerate((-1, 1)):
            wait_bytes(buf.at[1 + at], arecv.at[n, at])

            @pl.when(me.has_chain(step))
            def _():
                row_copy(at, arr, buf, step).start()

            @pl.when(jnp.logical_not(me.has_chain(step)))
            def _():
                buf[3 * at] = jnp.zeros(buf.shape[1:], BF16)

    for n, arr, buf, out in ((0, 0, hk, kt), (2, 1, hv, vt)):
        pass_rows(n, arr, buf)
        for a in (1, 2):
            flip_row(buf, out, a)
    for n, buf in ((1, hq), (3, hg)):
        for at in range(2):
            wait_bytes(buf.at[at], arecv.at[n, at])

    head = me.x * NY + me.y

    def tile_copy(act, n, src, land, r, j):
        dev = (NX * me.z + 2 * me.c + r, j)
        is_self = (dev[0] == me.tr) & (me.tc == j)
        act(is_self, src.at[r, j], land.at[head], dsend.at[n, r, j], drecv.at[n], dev)

    def edge_copy(arr, r, pair, step):
        view = pl.ds(2 * pair, 2)
        return remote(
            edge.at[arr, r, view], elan.at[arr, 1 - r, view],
            esend.at[arr, r, pair], erecv.at[arr, r], me.chain(step),
        )

    def halves(t):
        return slice(t * TOK, (t + 1) * TOK)

    def scores(i):
        r, j, par = i // 4, 2 * (i % 4), i % 2
        qs = [hq[r, j], hq[r, j + 1]]
        gs = [hg[r, j], hg[r, j + 1]]
        q2 = jnp.concatenate(qs, axis=1)
        g2 = jnp.concatenate(gs, axis=1)
        dead = q2[HEAD_DIM:].astype(F32)
        far = jnp.where(me.has_chain(2 * r - 1), 0.0, BIG)
        top = jnp.full((8, 2 * TOK), -3.0e38, F32)
        for p in range(TC + 2):
            if p < TC:
                s_buf[par, p] = dot(kt[1 + r, p], q2, 1, 0)
                g_buf[par, p] = dot(vt[1 + r, p], g2, 1, 0)
                bias = dead[p : p + 1]
            else:
                a = r + 2 * (p - TC)
                for t in range(2):
                    s_buf[par, p, :, halves(t)] = dot(kt[a, j + t], qs[t], 1, 0)
                    g_buf[par, p, :, halves(t)] = dot(vt[a, j + t], gs[t], 1, 0)
                bias = far if a in (0, 3) else 0.0
            top = jnp.maximum(top, jnp.max(s_buf[par, p].reshape(TOK // 8, 8, 2 * TOK), axis=0) - bias)
        top_buf[par] = top

    def soften(i):
        r, j, par = i // 4, 2 * (i % 4), i % 2
        q2 = jnp.concatenate([hq[r, j], hq[r, j + 1]], axis=1).astype(F32)
        g2 = jnp.concatenate([hg[r, j], hg[r, j + 1]], axis=1).astype(F32)
        dead = q2[HEAD_DIM:]
        far = jnp.where(me.has_chain(2 * r - 1), 0.0, BIG)
        top = jnp.max(top_buf[par], axis=0, keepdims=True) * EXP_SCALE
        total = jnp.zeros((8, 2 * TOK), F32)
        delta = jnp.zeros((8, 2 * TOK), F32)
        for p in range(TC + 2):
            if p < TC:
                shift = top + dead[p : p + 1]
            else:
                shift = top + far if r + 2 * (p - TC) in (0, 3) else top
            e = jnp.exp2(s_buf[par, p] * EXP_SCALE - shift)
            s_buf[par, p] = e
            e_buf[par, p] = e.astype(BF16)
            total = total + jnp.sum(e.reshape(TOK // 8, 8, 2 * TOK), axis=0)
            delta = delta + jnp.sum((e * g_buf[par, p]).reshape(TOK // 8, 8, 2 * TOK), axis=0)
        inv = 1.0 / jnp.sum(total, axis=0, keepdims=True)
        delta = jnp.sum(delta, axis=0, keepdims=True) * inv
        for p in range(TC + 2):
            d_buf[par, p] = (s_buf[par, p] * (g_buf[par, p] - delta)).astype(BF16)
        scaled = inv * ROOT
        inv_buf[par] = jnp.broadcast_to(scaled, (8, 2 * TOK))
        qn_buf[par] = (q2 * scaled).astype(BF16)
        gn_buf[par] = (g2 * inv).astype(BF16)

    def grads(i):
        r, j, par = i // 4, 2 * (i % 4), i % 2
        qn = qn_buf[par]
        gn = gn_buf[par]

        def add(acc, at, tile, value, first):
            acc[at, tile] = value if first else acc[at, tile] + value

        ds_row = jnp.concatenate([d_buf[par, p] for p in range(TC)], axis=0)
        e_row = jnp.concatenate([e_buf[par, p] for p in range(TC)], axis=0)
        dq = dot(jnp.concatenate([hk[1 + r, p] for p in range(TC)], axis=1), ds_row, 1, 0)
        key_row = dot(qn, ds_row, 1, 1)
        value_row = dot(gn, e_row, 1, 1)
        for p in range(TC):
            add(acc_k, r, p, key_row[:, halves(p)], i == 0)
            add(acc_v, r, p, value_row[:, halves(p)], i == 0)
        parts = []
        for t in range(2):
            part = jnp.zeros((PAD_DIM, TOK), F32)
            for p in range(TC, TC + 2):
                a = r + 2 * (p - TC)
                ds = d_buf[par, p, :, halves(t)]
                part = part + dot(hk[a, j + t], ds, 1, 0)
                key_term = dot(qn[:, halves(t)], ds, 1, 1)
                value_term = dot(gn[:, halves(t)], e_buf[par, p, :, halves(t)], 1, 1)
                if a in (0, 3):
                    edge[0, r, j + t] = key_term.astype(BF16)
                    edge[1, r, j + t] = value_term.astype(BF16)
                else:
                    add(acc_k, 1 - r, j + t, key_term, r == 0)
                    add(acc_v, 1 - r, j + t, value_term, r == 0)
            parts.append(part)
        dq = ((dq + jnp.concatenate(parts, axis=1)) * inv_buf[par, 0:1]).astype(BF16)
        tq[r, j] = dq[:, :TOK]
        tq[r, j + 1] = dq[:, TOK:]

    def send_terms(i):
        r, pair = i // 4, i % 4
        step = 2 * r - 1

        @pl.when(me.has_chain(step))
        def _():
            edge_copy(1, r, pair, step).start()
            edge_copy(0, r, pair, step).start()

        for t in range(2):
            tile_copy(start_or_local, 0, tq, lq, r, 2 * pair + t)

    def take_outer(r):
        step = 2 * r - 1
        for arr, buf in ((0, hk), (1, hv)):

            @pl.when(me.has_chain(step))
            def _():
                row_copy(1 - r, arr, buf, -step).wait_recv()

        flip_row(hk, kt, 3 * r)
        flip_row(hv, vt, 3 * r)

    visits = TC
    take_outer(0)
    scores(0)
    for i in range(visits + 1):
        if i + 1 == visits // 2:
            take_outer(1)
        if i >= 1:
            grads(i - 1)
        if i < visits:
            soften(i)
        if i + 1 < visits:
            scores(i + 1)
        if i >= 1:
            send_terms(i - 1)
        if i == 1:
            pass_rows(4, 2, hc)

    for arr, n, acc, out, land in ((1, 2, acc_v, tv, lv), (0, 1, acc_k, tk, lk)):
        for r, step in ((1, 1), (0, -1)):

            @pl.when(me.has_chain(step))
            def _():
                wait_bytes(elan.at[arr, r], erecv.at[arr, 1 - r])

            extra = jnp.where(me.has_chain(step), elan[arr, r].astype(F32), 0.0)
            for j in range(TC):
                out[r, j] = (acc[r, j] + extra[j]).astype(BF16)
            for j in range(TC):
                tile_copy(start_or_local, n, out, land, r, j)

    for step in (-1, 1):

        @pl.when(me.has_chain(step))
        def _():
            row_copy((1 - step) // 2, 2, hc, -step).wait_recv()

    lane = lax.broadcasted_iota(jnp.int32, (PAD_DIM, TOK), 1)
    low = lane < TOK // 2
    first = lane % 64 == 0
    last = lane % 64 == 63
    blank = jnp.zeros((PAD_DIM, TOK), F32)
    for a in range(3):
        for r in range(2):
            taps[a, r, 0] = blank
            taps[a, r, TC + 1] = blank

    def shift_rows(j, _):
        for r in range(2):
            own = hc[1 + r, j].astype(F32)
            taps[0, r, j + 1] = pltpu.roll(jnp.where(low, own, hc[r, j].astype(F32)), 64, 1)
            taps[1, r, j + 1] = own
            taps[2, r, j + 1] = pltpu.roll(jnp.where(low, hc[2 + r, j].astype(F32), own), 64, 1)
        return 0

    lax.fori_loop(0, TC, shift_rows, 0)
    table = blank
    for a in range(3):

        def add_tile(j, sums):
            for r in range(2):
                gv = tv[r, j].astype(F32)
                here = taps[a, r, j + 1]
                left = jnp.where(first, pltpu.roll(taps[a, r, j], 65, 1), pltpu.roll(here, 1, 1))
                right = jnp.where(last, pltpu.roll(taps[a, r, j + 2], 63, 1), pltpu.roll(here, 127, 1))
                sums = (sums[0] + left * gv, sums[1] + here * gv, sums[2] + right * gv)
            return sums

        sums = lax.fori_loop(0, TC, add_tile, (blank, blank, blank))
        for b in range(3):
            table = jnp.where(lane == 3 * a + b, jnp.sum(sums[b], axis=1, keepdims=True), table)
    table = jnp.concatenate([table, jnp.zeros((TOK - PAD_DIM, TOK), F32)], axis=0)
    part1[...] = table.T[:16]

    def exchange(stage, count, mine, src, land, dev):
        def run(act):
            for other in range(count):
                act(mine == other, src, land.at[mine], psend.at[stage, other], precv.at[stage], dev(other))

        run(start_or_local)
        return run

    runs = [exchange(0, 2, me.c, part1, red1, lambda o: (me.tr, 2 * me.y + o))]

    for n, src, dst in ((0, sk, own_k), (1, sq, hq), (2, sv, own_v), (3, sg, hg), (4, sc, own_c)):
        head_copies(wait_sent, n, src, dst)

    def out_block(out):
        def put(b, x):
            out[:, :, b * 128 : b * 128 + 128] = x.reshape(2, 64, 128).astype(BF16)

        return put

    wait_bytes(lq, drecv.at[0])
    from_heads(lq, flip, out_block(oq))
    wait_bytes(red1, precv.at[0])
    part2[...] = jnp.sum(red1[...], axis=0)
    runs.append(exchange(1, NZ, me.z, part2, red2, lambda o: (NX * o + me.x, me.tc)))
    wait_bytes(lv, drecv.at[2])
    from_heads(lv, flip, out_block(ov))
    pack_rim(ov, gpack)
    halo_start(me, ov, gpack, grow, gcol, gdiag, gsend, grecv)
    wait_bytes(lk, drecv.at[1])
    from_heads(lk, flip, out_block(ok))
    wait_bytes(red2, precv.at[1])
    part3[...] = jnp.sum(red2[...], axis=0)
    runs.append(
        exchange(2, HEADS, head, part3, red3, lambda o: (NX * me.z + o // NY, 2 * (o % NY) + me.c))
    )
    for at, step in enumerate((-1, 1)):

        @pl.when(me.has_chain(step))
        def _():
            for arr, buf in ((0, hk), (1, hv), (2, hc)):
                row_copy(at, arr, buf, step).wait_send()
            for arr in range(2):
                for pair in range(TC // 2):
                    edge_copy(arr, at, pair, step).wait_send()

    for n, src, land in ((0, tq, lq), (1, tk, lk), (2, tv, lv)):
        for r in range(2):
            for j in range(TC):
                tile_copy(wait_sent, n, src, land, r, j)

    halo_wait(me, ov, gpack, grow, gcol, gdiag, gsend, grecv)
    fill_ext(me, ext, ov, grow, gcol, gdiag)
    for b in range(LANES):
        lanes = slice(b * 128, b * 128 + 128)
        total = jnp.zeros((2, 64, 128), F32)
        for a in range(3):
            for s in range(3):
                total = total + w[a, s, lanes][None, None, :] * ext[2 - a : 4 - a, 9 - s : 73 - s, lanes]
        oc[:, :, lanes] = total.astype(BF16)

    wait_bytes(red3, precv.at[2])
    column = lax.broadcasted_iota(jnp.int32, (16, TOK), 1)
    blocks = [jnp.zeros((16, TOK), F32) for _ in range(LANES)]
    for h in range(HEADS):
        b, off = h * HEAD_DIM // 128, h * HEAD_DIM % 128
        piece = pltpu.roll(red3[h], off, 1) if off else red3[h]
        blocks[b] = blocks[b] + jnp.where(column >= off, piece, 0.0)
        if off + HEAD_DIM > 128:
            blocks[b + 1] = blocks[b + 1] + jnp.where(column < off, piece, 0.0)
    for b in range(LANES):
        for tap in range(9):
            ow[tap // 3, tap % 3 : tap % 3 + 1, b * 128 : b * 128 + 128] = blocks[b][tap : tap + 1]
    for run in runs:
        run(wait_sent)


def copy_kernel(*refs):
    n = len(refs) // 2
    for src, dst in zip(refs[:n], refs[n:]):
        dst[...] = src[...]


def vmem_specs(n):
    return [pl.BlockSpec(memory_space=pltpu.VMEM)] * n


def per_device(query, key, value, control, kernel, grad_out, detail_blocks):
    sem = pltpu.SemaphoreType.DMA
    vm = pltpu.VMEM
    img = jax.ShapeDtypeStruct((2, 64, D), BF16)
    outs = (img, img, img, img, jax.ShapeDtypeStruct((3, 3, D), F32))
    rows = lambda n, t=BF16: vm((n, TC, PAD_DIM, TOK), t)
    tiles = vm((HEADS, PAD_DIM, TOK), BF16)
    halo = [vm((2, 2, 16, TOK), F32), vm((2, 64, D), BF16), vm((2, 2, 16, TOK), F32), vm((4, 16, TOK), F32)]
    pair = lambda t: vm((2, TC + 2, TOK, 2 * TOK), t)
    wide = vm((2, 8, 2 * TOK), F32)
    reduced = lambda n: vm((n, 16, TOK), F32)
    results = pl.pallas_call(
        whole_kernel,
        out_shape=outs,
        in_specs=[pl.BlockSpec(memory_space=pl.ANY)] * 5 + vmem_specs(1) + [pl.BlockSpec(memory_space=pltpu.SMEM)],
        out_specs=tuple(vmem_specs(5)),
        scratch_shapes=[vm((2, 64, D), BF16)] * 5
        + [rows(2), rows(2), rows(4), rows(4), rows(4)]
        + [tiles] * 5
        + [vm((D, TOK), F32), vm((4, 80, D), F32), vm((4, 80, D), F32)]
        + halo
        + halo
        + [vm((4, TC, TOK, PAD_DIM), BF16)] * 2
        + [pair(F32), pair(F32), pair(BF16), pair(BF16), wide, wide]
        + [vm((2, PAD_DIM, 2 * TOK), BF16)] * 2
        + [rows(2, F32)] * 2
        + [rows(2)] * 3
        + [vm((2, 2, TC, PAD_DIM, TOK), BF16)] * 2
        + [tiles] * 3
        + [vm((3, 2, TC + 2, PAD_DIM, TOK), F32), reduced(2), reduced(NZ), reduced(HEADS)]
        + [vm((16, TOK), F32)] * 3
        + [sem((5,)), sem((5, HEADS)), sem((5, 2)), sem((3, 2)), sem((3, 2))]
        + [sem((8,))] * 4
        + [sem((2, 2, 4)), sem((2, 2)), sem((3, 2, TC)), sem((3,)), sem((3, HEADS)), sem((3,))],
        compiler_params=pltpu.CompilerParams(collective_id=0, has_side_effects=True),
        name="whole",
    )(query, key, value, grad_out, control, kernel, detail_blocks)
    return pl.pallas_call(
        copy_kernel,
        out_shape=outs,
        in_specs=vmem_specs(5),
        out_specs=tuple(vmem_specs(5)),
        name="finish",
    )(*results)


def solution(mesh):
    tile = P("trow", "tcol", None)
    return jax.shard_map(
        per_device,
        mesh=mesh,
        in_specs=(tile, tile, tile, tile, P(), tile, P("trow", None, None)),
        out_specs=(tile, tile, tile, tile, P()),
        check_vma=False,
    )
```
